512 devices in a mesh: tx: 8 (over x, core), ty: 16 (over z), tz: 4 (over y).
Axes of the slice: x: 4, y: 4, z: 16, core: 2. Of those that a mesh axis runs over, the one named last changes fastest.
Arguments:
- start_block: float32 [64, 1048576], P(None, ('tx', 'ty', 'tz'))
- weights: bfloat16 [8192, 6, 128, 128], P(('tx', 'ty', 'tz')), may hold values from 0 to 0.25, as said below
- neighbours: int32 [8192, 6], P(('tx', 'ty', 'tz')), may hold values from 0 to 123, as said below
- boundary: int32 [2048], P(('tx', 'ty', 'tz')), may hold values from 0 to 15, as said below
Outputs:
- basis: float32 [64, 1048576], P(None, ('tx', 'ty', 'tz'))
- rfactor: float32 [64, 64], replicated
The draws below stay inside these ranges and needn't reach their ends.
Inputs may be any that keep to these rules, and one draw needn't show every extreme that they name: `neighbours`: slot 0 of block row b is b % 16; in the last of each device's 16 rows slot 1 is 123. `boundary`: each device's 4 entries are distinct, the last of them 16 - 1. For each block row b and point p, exactly 16 of the entries weights[b, s, q, p] over all slots s and rows q are nonzero, each positive.
All inputs are finite; a program needn't handle non-finite values.
Results may differ from the reference program's by a relative error of at most 0.00075.
Values may be sent and summed in bfloat16 or wider, within the bound.
No kernel may reach another device: no remote copies, remote signals or barrier semaphores. Data moves between devices by JAX's collectives and lax.ppermute only.
A program may use at most 64 MiB of HBM per device.

```python
import jax
import jax.numpy as jnp
from jax import lax

K = 64
B = 128
NBR = 6
KNN = 16
BLK_DEV = 16
BND = 4
NBLK = 8192
NPTS = 1048576
N_TX = 8
N_TY = 16
N_TZ = 4
DEVICES = 512


def draw_start_block(key, part):
    key_main, key_rows, key_cols = jax.random.split(jax.random.fold_in(key, 11), 3)
    device_pos = (jnp.arange(NPTS) // (BLK_DEV * B)).astype(jnp.float32) / max(DEVICES - 1, 1)
    row_scale = jnp.exp(jax.random.uniform(key_rows, (K, 1)) * jnp.log(10.0))
    col_scale = jnp.exp(jax.random.uniform(key_cols, (NPTS,)) * jnp.log(10.0))
    values = jax.random.normal(key_main, (K, NPTS))
    rise = jnp.exp(device_pos * jnp.log(3.0))
    return (0.1 * values * row_scale * col_scale * rise).astype(jnp.float32)


def draw_weights(key, part):
    key_pick, key_value = jax.random.split(jax.random.fold_in(key, 53), 2)
    span = NBR * B // KNN
    chosen = jax.random.randint(key_pick, (NBLK, KNN, B), 0, span)
    spread = jnp.repeat(chosen, span, axis=1)
    flat_ids = jnp.arange(NBR * B, dtype=jnp.int32)[None, :, None] % span
    keep = (spread == flat_ids).astype(jnp.float32)
    values = jnp.exp(jax.random.uniform(key_value, (NBLK, NBR * B, B), minval=jnp.log(0.05), maxval=jnp.log(0.25)))
    return (values * keep).reshape(NBLK, NBR, B, B).astype(jnp.bfloat16)


def draw_neighbours(key, part):
    picks = jax.random.randint(jax.random.fold_in(key, 23), (NBLK, NBR), 0, BLK_DEV + 27 * BND)
    row_ids = jnp.arange(NBLK, dtype=jnp.int32)
    picks = picks.at[:, 0].set(row_ids % BLK_DEV)
    last_row = row_ids % BLK_DEV == BLK_DEV - 1
    picks = picks.at[:, 1].set(jnp.where(last_row, BLK_DEV + 27 * BND - 1, picks[:, 1]))
    return picks.astype(jnp.int32)


def draw_boundary(key, part):
    device_keys = jax.random.split(jax.random.fold_in(key, 37), DEVICES)

    def one_list(device_key):
        chosen = jax.random.permutation(device_key, BLK_DEV - 1)[:BND - 1]
        return jnp.concatenate([chosen.astype(jnp.int32), jnp.full((1,), BLK_DEV - 1, jnp.int32)])
    return jax.vmap(one_list)(device_keys).reshape(-1).astype(jnp.int32)


def setup_inputs(seed: int = 0) -> dict:
    arg_keys = jax.random.split(jax.random.key(seed), 5)
    start_block = draw_start_block(jax.random.fold_in(arg_keys[4], 71), 0)
    weights = draw_weights(jax.random.fold_in(arg_keys[4], 71), 0)
    neighbours = draw_neighbours(jax.random.fold_in(arg_keys[4], 71), 0)
    boundary = draw_boundary(jax.random.fold_in(arg_keys[4], 71), 0)
    return {"start_block": start_block, "weights": weights, "neighbours": neighbours, "boundary": boundary}


def source_blocks(neighbours, boundary):
    device_ids = jnp.arange(DEVICES, dtype=jnp.int32)[:, None, None]
    listed = neighbours.reshape(DEVICES, BLK_DEV, NBR)
    coord_x = device_ids // (N_TY * N_TZ)
    coord_y = device_ids // N_TZ % N_TY
    coord_z = device_ids % N_TZ
    remote = jnp.maximum(listed - BLK_DEV, 0)
    offset = remote // BND
    position = remote % BND
    other_x = coord_x + offset // 9 - 1
    other_y = coord_y + offset // 3 % 3 - 1
    other_z = coord_z + offset % 3 - 1
    inside = (other_x >= 0) & (other_x < N_TX) & (other_y >= 0) & (other_y < N_TY) & (other_z >= 0) & (other_z < N_TZ)
    partner = (jnp.clip(other_x, 0, N_TX - 1) * N_TY + jnp.clip(other_y, 0, N_TY - 1)) * N_TZ + jnp.clip(other_z, 0, N_TZ - 1)
    far_block = partner * BLK_DEV + boundary[partner * BND + position]
    own_slot = listed < BLK_DEV
    source = jnp.where(own_slot, device_ids * BLK_DEV + listed, far_block).astype(jnp.int32)
    return (source, own_slot | inside)

def apply_operator(current, degree, weights, source, live):
    rounded = current.astype(jnp.bfloat16).reshape(K, NBLK, B)
    tiles = weights.reshape(DEVICES, BLK_DEV, NBR, B, B)

    def one_device(members):
        source_ids, live_mask, tile_set = members
        picked = jnp.take(rounded, source_ids, axis=1).astype(jnp.float32)
        picked = picked * live_mask[None, :, :, None].astype(jnp.float32)
        return jnp.einsum('kisq,isqp->kip', picked, tile_set.astype(jnp.float32))
    products = lax.map(one_device, (source, live, tiles))
    product = jnp.transpose(products, (1, 0, 2, 3)).reshape(K, NPTS)
    return current * (1.0 - degree * 0.125) + product * 0.125

def lower_factor(mixed):
    gram = jnp.dot(mixed.astype(jnp.float32), mixed.T.astype(jnp.float32), precision=lax.Precision.HIGHEST, preferred_element_type=jnp.float32)
    return jnp.linalg.cholesky(gram)

def reference(start_block, weights, neighbours, boundary):
    source, live = source_blocks(neighbours, boundary)
    degree = jnp.sum(weights.astype(jnp.float32), axis=(1, 2)).reshape(NPTS)
    root_scale = float(NPTS) ** 0.5
    current = start_block
    lower = None
    for section_index in range(2):
        mixed = apply_operator(current, degree, weights, source, live)
        lower = lower_factor(mixed)
        current = lax.linalg.triangular_solve(lower, mixed, left_side=True, lower=True) * root_scale
    return (current, lower.T / root_scale)
```

```python
import functools

import jax
import jax.numpy as jnp
from jax import lax
from jax.experimental import pallas as pl
from jax.experimental.pallas import tpu as pltpu
from jax.sharding import PartitionSpec as P

F32 = jnp.float32
BF16 = jnp.bfloat16
HIGHEST = lax.Precision.HIGHEST
PLANE = ("tx", "tz")
MIB = 1 << 20


def vmem():
    return pl.BlockSpec(memory_space=pltpu.VMEM)


def smem():
    return pl.BlockSpec(memory_space=pltpu.SMEM)


def anywhere():
    return pl.BlockSpec(memory_space=pl.ANY)


def dot_nt(a, b):
    return lax.dot_general(
        a, b, (((1,), (1,)), ((), ())), precision=HIGHEST, preferred_element_type=F32
    )


def edge_kernel(bnd_ref, x_ref, edge_ref, held, sem):
    count = edge_ref.shape[0]
    copies = []
    for j in range(count):
        start = pl.multiple_of(bnd_ref[j] * 128, 128)
        copies.append(
            pltpu.make_async_copy(x_ref.at[:, pl.ds(start, 128)], held.at[j], sem.at[j])
        )
        copies[-1].start()
    for j in range(count):
        copies[j].wait()
        edge_ref[j] = held[j].astype(BF16)


def take_edges(boundary, start_block):
    count = boundary.shape[0]
    width = start_block.shape[0]
    return pl.pallas_call(
        edge_kernel,
        out_shape=jax.ShapeDtypeStruct((count, width, 128), BF16),
        in_specs=[smem(), anywhere()],
        out_specs=vmem(),
        scratch_shapes=[
            pltpu.VMEM((count, width, 128), F32),
            pltpu.SemaphoreType.DMA((count,)),
        ],
        name="edges",
    )(boundary, start_block)


def neighbours_along(block, axis):
    count = lax.axis_size(axis)
    forward = [(i, i + 1) for i in range(count - 1)]
    backward = [(target, source) for source, target in forward]
    return lax.ppermute(block, axis, forward), lax.ppermute(block, axis, backward)


def halo(edge):
    block = edge
    for axis in ("tz", "ty"):
        low, high = neighbours_along(block, axis)
        block = jnp.concatenate([low, block, high], axis=0)
    low, high = neighbours_along(block, "tx")
    return low, block, high


def start_fill(far_refs, pool, base, sem):
    copies = []
    for j, ref in enumerate(far_refs):
        count = ref.shape[0]
        copies.append(
            pltpu.make_async_copy(ref, pool.at[pl.ds(base + j * count, count)], sem.at[j])
        )
        copies[-1].start()
    return copies


def first_kernel(
    nbr_ref, bnd_ref, x_ref, w_ref, low_ref, mid_ref, high_ref,
    mixed_ref, split_ref, edge_ref, keep_ref, pool, sem,
):
    blocks, slots = nbr_ref.shape
    width = x_ref.shape[0]
    fills = start_fill((low_ref, mid_ref, high_ref), pool, blocks, sem)
    for i in range(blocks):
        pool[i] = x_ref[:, i * 128:(i + 1) * 128].astype(BF16)
    for copy in fills:
        copy.wait()
    ones = jnp.ones((16, slots * 128), BF16)
    for i in range(blocks):
        picked = jnp.concatenate([pool[nbr_ref[i, s]] for s in range(slots)], axis=1)
        both = jnp.concatenate([picked, ones], axis=0)
        out = jnp.dot(both, w_ref[i], preferred_element_type=F32)
        keep = 1.0 - out[width:width + 8] * 0.125
        keep_ref[i] = keep
        mixed = x_ref[:, i * 128:(i + 1) * 128] * keep[0:1] + out[:width] * 0.125
        mixed_ref[i] = mixed
        head = mixed.astype(BF16)
        split_ref[i, 0:width] = head
        split_ref[i, width:2 * width] = (mixed - head.astype(F32)).astype(BF16)
    for j in range(edge_ref.shape[0]):
        edge_ref[j] = split_ref[bnd_ref[j]]


def first_step(neighbours, boundary, start_block, weights, far):
    blocks, slots = neighbours.shape
    width = start_block.shape[0]
    total = blocks + 3 * far[0].shape[0]
    return pl.pallas_call(
        first_kernel,
        out_shape=(
            jax.ShapeDtypeStruct((blocks, width, 128), F32),
            jax.ShapeDtypeStruct((blocks, 2 * width, 128), BF16),
            jax.ShapeDtypeStruct((boundary.shape[0], 2 * width, 128), BF16),
            jax.ShapeDtypeStruct((blocks, 8, 128), F32),
        ),
        in_specs=[smem(), smem(), vmem(), vmem(), anywhere(), anywhere(), anywhere()],
        out_specs=(vmem(), vmem(), vmem(), vmem()),
        scratch_shapes=[
            pltpu.VMEM((total, width, 128), BF16),
            pltpu.SemaphoreType.DMA((3,)),
        ],
        compiler_params=pltpu.CompilerParams(vmem_limit_bytes=24 * MIB),
        name="first_step",
    )(neighbours, boundary, start_block, weights, *far)


def gram_kernel(mixed_ref, gram_ref):
    total = None
    for i in range(mixed_ref.shape[0]):
        part = dot_nt(mixed_ref[i], mixed_ref[i])
        total = part if total is None else total + part
    gram_ref[...] = total


def local_gram(mixed):
    blocks, width, _ = mixed.shape
    return pl.pallas_call(
        gram_kernel,
        out_shape=jax.ShapeDtypeStruct((width, width), F32),
        in_specs=[vmem()],
        out_specs=vmem(),
        compiler_params=pltpu.CompilerParams(vmem_limit_bytes=8 * MIB),
        cost_estimate=pl.CostEstimate(
            flops=12 * blocks * 128 * width * width,
            bytes_accessed=4 * blocks * 128 * width,
            transcendentals=0,
        ),
        name="first_gram",
    )(mixed)


def second_kernel(
    nbr_ref, mixed_ref, split_ref, keep_ref, w_ref, gram_ref, low_ref, mid_ref, high_ref,
    out_ref, both_ref, pool, sem,
):
    blocks, slots = nbr_ref.shape
    width = mixed_ref.shape[1]
    fills = start_fill((low_ref, mid_ref, high_ref), pool, blocks, sem)
    for i in range(blocks):
        pool[i] = split_ref[i]
    for copy in fills:
        copy.wait()
    total = None
    for i in range(blocks):
        picked = jnp.concatenate([pool[nbr_ref[i, s]] for s in range(slots)], axis=1)
        out = jnp.dot(picked, w_ref[i], preferred_element_type=F32)
        mixed = mixed_ref[i] * keep_ref[i, 0:1] + (out[:width] + out[width:]) * 0.125
        out_ref[i] = mixed
        part = dot_nt(mixed, mixed)
        total = part if total is None else total + part
    both_ref[...] = jnp.concatenate([gram_ref[...], total], axis=1)


def second_step(neighbours, mixed, split, keep, weights, gram, far):
    blocks, slots = neighbours.shape
    width = mixed.shape[1]
    total = blocks + 3 * far[0].shape[0]
    return pl.pallas_call(
        second_kernel,
        out_shape=(
            jax.ShapeDtypeStruct((blocks, width, 128), F32),
            jax.ShapeDtypeStruct((width, 2 * width), F32),
        ),
        in_specs=[smem()] + [vmem()] * 5 + [anywhere()] * 3,
        out_specs=(vmem(), vmem()),
        scratch_shapes=[
            pltpu.VMEM((total, 2 * width, 128), BF16),
            pltpu.SemaphoreType.DMA((3,)),
        ],
        compiler_params=pltpu.CompilerParams(vmem_limit_bytes=24 * MIB),
        name="second_step",
    )(neighbours, mixed, split, keep, weights, gram, *far)


def sum_over_devices(values):
    rows, lanes = values.shape
    plane = lax.axis_size("tx") * lax.axis_size("tz")
    line = lax.axis_size("ty")
    piece = rows // plane
    parts = lax.all_to_all(values.reshape(plane, piece, lanes), PLANE, 0, 0)
    mine = jnp.sum(parts, axis=0)
    parts = lax.all_to_all(jnp.broadcast_to(mine[None], (line, piece, lanes)), "ty", 0, 0)
    mine = jnp.sum(parts, axis=0)
    parts = lax.all_to_all(jnp.broadcast_to(mine[None], (plane, piece, lanes)), PLANE, 0, 0)
    return parts.reshape(rows, lanes)


def finish_kernel(root_scale, gram_ref, mixed_ref, basis_ref, rfactor_ref):
    width = gram_ref.shape[0]
    shape = (width, 2 * width)
    row_id = lax.broadcasted_iota(jnp.int32, shape, 0)
    lane_id = lax.broadcasted_iota(jnp.int32, shape, 1)
    first = lane_id < width
    upper = gram_ref[...]
    inverse = (jnp.where(first, lane_id, lane_id - width) == row_id).astype(F32)
    pivots = jnp.ones(shape, F32)
    for k in range(width):
        column = jnp.where(first, upper[:, k:k + 1], upper[:, width + k:width + k + 1])
        pivot = column[k:k + 1]
        pivots = jnp.where(row_id == k, pivot, pivots)
        factor = jnp.where(row_id > k, column * (1.0 / pivot), 0.0)
        upper = upper - factor * upper[k:k + 1]
        inverse = inverse - factor * inverse[k:k + 1]
    scale = lax.rsqrt(pivots)
    lower_t = (upper * scale)[:, width:]
    inverse = inverse * scale
    rid = lax.broadcasted_iota(jnp.int32, (width, width), 0)
    cid = lax.broadcasted_iota(jnp.int32, (width, width), 1)
    lower_t = jnp.where(cid >= rid, lower_t, 0.0)
    rfactor = dot_nt(lower_t, inverse[:, :width])
    rfactor_ref[...] = jnp.where(cid >= rid, rfactor, 0.0)
    solve = inverse[:, width:] * root_scale
    for i in range(mixed_ref.shape[0]):
        basis_ref[:, i * 128:(i + 1) * 128] = jnp.dot(
            solve, mixed_ref[i], precision=HIGHEST, preferred_element_type=F32
        )


def finish(gram, mixed, root_scale):
    blocks, width, lanes = mixed.shape
    return pl.pallas_call(
        functools.partial(finish_kernel, root_scale),
        out_shape=(
            jax.ShapeDtypeStruct((width, blocks * lanes), F32),
            jax.ShapeDtypeStruct((width, width), F32),
        ),
        in_specs=[vmem(), vmem()],
        out_specs=(vmem(), vmem()),
        compiler_params=pltpu.CompilerParams(vmem_limit_bytes=16 * MIB),
        name="finish",
    )(gram, mixed)


def per_device(start_block, weights, neighbours, boundary):
    points = start_block.shape[1]
    blocks, slots, size, _ = weights.shape
    devices = lax.axis_size("tx") * lax.axis_size("ty") * lax.axis_size("tz")
    root_scale = float(points * devices) ** 0.5
    tiles = weights.reshape(blocks, slots * size, size)
    far = halo(take_edges(boundary, start_block))
    mixed, split, edge, keep = first_step(neighbours, boundary, start_block, tiles, far)
    far = halo(edge)
    gram = local_gram(mixed)
    mixed, both = second_step(neighbours, mixed, split, keep, tiles, gram, far)
    return finish(sum_over_devices(both), mixed, root_scale)


def solution(mesh):
    placed = (
        P(None, ("tx", "ty", "tz")),
        P(("tx", "ty", "tz"), None, None, None),
        P(("tx", "ty", "tz"), None),
        P(("tx", "ty", "tz")),
    )
    return jax.shard_map(
        per_device,
        mesh=mesh,
        in_specs=placed,
        out_specs=(P(None, ("tx", "ty", "tz")), P()),
        check_vma=False,
    )
```

```python
import functools

import jax
import jax.numpy as jnp
from jax import lax
from jax.experimental import pallas as pl
from jax.experimental.pallas import tpu as pltpu
from jax.sharding import PartitionSpec as P

F32 = jnp.float32
BF16 = jnp.bfloat16
HIGHEST = lax.Precision.HIGHEST
PLANE = ("tx", "tz")
MIB = 1 << 20
PANEL = 8


def vmem():
    return pl.BlockSpec(memory_space=pltpu.VMEM)


def smem():
    return pl.BlockSpec(memory_space=pltpu.SMEM)


def anywhere():
    return pl.BlockSpec(memory_space=pl.ANY)


def in_hbm(array):
    return pltpu.with_memory_space_constraint(array, pltpu.HBM)


def dot_nt(a, b):
    return lax.dot_general(
        a, b, (((1,), (1,)), ((), ())), precision=HIGHEST, preferred_element_type=F32
    )


def edge_kernel(list_ref, x_ref, edge_ref, bnd_ref, held, list_sem, sem):
    count = edge_ref.shape[0]
    listing = pltpu.make_async_copy(list_ref, bnd_ref, list_sem)
    listing.start()
    listing.wait()
    copies = []
    for j in range(count):
        start = pl.multiple_of(bnd_ref[j] * 128, 128)
        copies.append(
            pltpu.make_async_copy(x_ref.at[:, pl.ds(start, 128)], held.at[j], sem.at[j])
        )
        copies[-1].start()
    for j in range(count):
        copies[j].wait()
        edge_ref[j] = held[j].astype(BF16)


def take_edges(boundary, start_block):
    count = boundary.shape[0]
    width = start_block.shape[0]
    return pl.pallas_call(
        edge_kernel,
        out_shape=jax.ShapeDtypeStruct((count, width, 128), BF16),
        in_specs=[anywhere(), anywhere()],
        out_specs=vmem(),
        scratch_shapes=[
            pltpu.SMEM((count,), jnp.int32),
            pltpu.VMEM((count, width, 128), F32),
            pltpu.SemaphoreType.DMA,
            pltpu.SemaphoreType.DMA((count,)),
        ],
        compiler_params=pltpu.CompilerParams(vmem_limit_bytes=2 * MIB),
        name="edges",
    )(in_hbm(boundary), in_hbm(start_block))


def hold_kernel(w_ref, held_ref, sem):
    copy = pltpu.make_async_copy(w_ref, held_ref, sem)
    copy.start()
    copy.wait()


def hold_weights(tiles):
    return pl.pallas_call(
        hold_kernel,
        out_shape=jax.ShapeDtypeStruct(tiles.shape, tiles.dtype),
        in_specs=[anywhere()],
        out_specs=vmem(),
        scratch_shapes=[pltpu.SemaphoreType.DMA],
        compiler_params=pltpu.CompilerParams(vmem_limit_bytes=8 * MIB),
        cost_estimate=pl.CostEstimate(
            flops=0, bytes_accessed=4 * tiles.size, transcendentals=0
        ),
        name="hold_weights",
    )(in_hbm(tiles))


def neighbours_along(block, axis):
    count = lax.axis_size(axis)
    forward = [(i, i + 1) for i in range(count - 1)]
    backward = [(target, source) for source, target in forward]
    return lax.ppermute(block, axis, forward), lax.ppermute(block, axis, backward)


def halo(edge):
    block = edge
    for axis in ("tz", "ty"):
        low, high = neighbours_along(block, axis)
        block = jnp.concatenate([low, block, high], axis=0)
    low, high = neighbours_along(block, "tx")
    return low, block, high


def start_fill(far_refs, pool, base, sem):
    copies = []
    for j, ref in enumerate(far_refs):
        count = ref.shape[0]
        copies.append(
            pltpu.make_async_copy(ref, pool.at[pl.ds(base + j * count, count)], sem.at[j])
        )
        copies[-1].start()
    return copies


def first_kernel(
    nbr_ref, bnd_ref, x_ref, w_ref, low_ref, mid_ref, high_ref,
    mixed_ref, split_ref, edge_ref, keep_ref, pool, sem,
):
    blocks, slots = nbr_ref.shape
    width = x_ref.shape[0]
    fills = start_fill((low_ref, mid_ref, high_ref), pool, blocks, sem)
    for i in range(blocks):
        pool[i] = x_ref[:, i * 128:(i + 1) * 128].astype(BF16)
    for copy in fills:
        copy.wait()
    ones = jnp.ones((16, slots * 128), BF16)
    for i in range(blocks):
        picked = jnp.concatenate([pool[nbr_ref[i, s]] for s in range(slots)], axis=1)
        both = jnp.concatenate([picked, ones], axis=0)
        out = jnp.dot(both, w_ref[i], preferred_element_type=F32)
        keep = 1.0 - out[width:width + 8] * 0.125
        keep_ref[i] = keep
        mixed = x_ref[:, i * 128:(i + 1) * 128] * keep[0:1] + out[:width] * 0.125
        mixed_ref[i] = mixed
        head = mixed.astype(BF16)
        split_ref[i, 0:width] = head
        split_ref[i, width:2 * width] = (mixed - head.astype(F32)).astype(BF16)
    for j in range(edge_ref.shape[0]):
        edge_ref[j] = split_ref[bnd_ref[j]]


def first_step(neighbours, boundary, start_block, weights, far):
    blocks, slots = neighbours.shape
    width = start_block.shape[0]
    total = blocks + 3 * far[0].shape[0]
    return pl.pallas_call(
        first_kernel,
        out_shape=(
            jax.ShapeDtypeStruct((blocks, width, 128), F32),
            jax.ShapeDtypeStruct((blocks, 2 * width, 128), BF16),
            jax.ShapeDtypeStruct((boundary.shape[0], 2 * width, 128), BF16),
            jax.ShapeDtypeStruct((blocks, 8, 128), F32),
        ),
        in_specs=[smem(), smem(), vmem(), vmem(), anywhere(), anywhere(), anywhere()],
        out_specs=(vmem(), vmem(), vmem(), vmem()),
        scratch_shapes=[
            pltpu.VMEM((total, width, 128), BF16),
            pltpu.SemaphoreType.DMA((3,)),
        ],
        compiler_params=pltpu.CompilerParams(vmem_limit_bytes=24 * MIB),
        name="first_step",
    )(neighbours, boundary, start_block, weights, *far)


def gram_kernel(mixed_ref, gram_ref):
    total = None
    for i in range(mixed_ref.shape[0]):
        part = dot_nt(mixed_ref[i], mixed_ref[i])
        total = part if total is None else total + part
    gram_ref[...] = total


def local_gram(mixed):
    blocks, width, _ = mixed.shape
    return pl.pallas_call(
        gram_kernel,
        out_shape=jax.ShapeDtypeStruct((width, width), F32),
        in_specs=[vmem()],
        out_specs=vmem(),
        compiler_params=pltpu.CompilerParams(vmem_limit_bytes=8 * MIB),
        cost_estimate=pl.CostEstimate(
            flops=12 * blocks * 128 * width * width,
            bytes_accessed=4 * blocks * 128 * width,
            transcendentals=0,
        ),
        name="first_gram",
    )(mixed)


def second_kernel(
    nbr_ref, mixed_ref, split_ref, keep_ref, w_ref, gram_ref, low_ref, mid_ref, high_ref,
    out_ref, both_ref, pool, wide, sem,
):
    blocks, slots = nbr_ref.shape
    width = mixed_ref.shape[1]
    fills = start_fill((low_ref, mid_ref, high_ref), pool, blocks, sem)
    for i in range(blocks):
        pool[i] = split_ref[i]
    for copy in fills:
        copy.wait()
    for i in range(blocks):
        picked = jnp.concatenate([pool[nbr_ref[i, s]] for s in range(slots)], axis=1)
        out = jnp.dot(picked, w_ref[i], preferred_element_type=F32)
        mixed = mixed_ref[i] * keep_ref[i, 0:1] + (out[:width] + out[width:]) * 0.125
        out_ref[i] = mixed
        wide[:, i * 128:(i + 1) * 128] = mixed
    both_ref[...] = jnp.concatenate([gram_ref[...], dot_nt(wide[...], wide[...])], axis=1)


def second_step(neighbours, mixed, split, keep, weights, gram, far):
    blocks, slots = neighbours.shape
    width = mixed.shape[1]
    total = blocks + 3 * far[0].shape[0]
    return pl.pallas_call(
        second_kernel,
        out_shape=(
            jax.ShapeDtypeStruct((blocks, width, 128), F32),
            jax.ShapeDtypeStruct((width, 2 * width), F32),
        ),
        in_specs=[smem()] + [vmem()] * 5 + [anywhere()] * 3,
        out_specs=(vmem(), vmem()),
        scratch_shapes=[
            pltpu.VMEM((total, 2 * width, 128), BF16),
            pltpu.VMEM((width, blocks * 128), F32),
            pltpu.SemaphoreType.DMA((3,)),
        ],
        compiler_params=pltpu.CompilerParams(vmem_limit_bytes=24 * MIB),
        name="second_step",
    )(neighbours, mixed, split, keep, weights, gram, *far)


def sum_over_devices(values):
    rows, lanes = values.shape
    plane = lax.axis_size("tx") * lax.axis_size("tz")
    line = lax.axis_size("ty")
    piece = rows // plane
    parts = lax.all_to_all(values.reshape(plane, piece, lanes), PLANE, 0, 0)
    mine = jnp.sum(parts, axis=0)
    parts = lax.all_to_all(jnp.broadcast_to(mine[None], (line, piece, lanes)), "ty", 0, 0)
    mine = jnp.sum(parts, axis=0)
    parts = lax.all_to_all(jnp.broadcast_to(mine[None], (plane, piece, lanes)), PLANE, 0, 0)
    return parts.reshape(rows, lanes)


def finish_kernel(root_scale, gram_ref, mixed_ref, basis_ref, rfactor_ref):
    width, lanes = gram_ref.shape
    tiles = width // PANEL
    lane = lax.broadcasted_iota(jnp.int32, (PANEL, lanes), 1)
    row = lax.broadcasted_iota(jnp.int32, (PANEL, lanes), 0)
    first = lane < width
    own = jnp.where(first, lane, lane - width)
    upper = [gram_ref[t * PANEL:(t + 1) * PANEL, :] for t in range(tiles)]
    inverse = [(own == row + t * PANEL).astype(F32) for t in range(tiles)]
    pivots = []

    def spread_row(tile, r):
        return jnp.broadcast_to(tile[r:r + 1], tile.shape)

    for p in range(tiles):
        columns = []
        for j in range(PANEL):
            lane_of = jnp.where(first, 0, width) + (p * PANEL + j)
            columns.append([
                jnp.take_along_axis(upper[t], lane_of, axis=1, mode="promise_in_bounds")
                if t >= p else None
                for t in range(tiles)
            ])
        corner = [[spread_row(columns[j][p], i) for j in range(i + 1)] for i in range(PANEL)]
        up_rows = [spread_row(upper[p], j) for j in range(PANEL)]
        inv_rows = [spread_row(inverse[p], j) for j in range(PANEL)]
        factor = [[None] * PANEL for _ in range(PANEL)]
        recip = []
        pivot = corner[0][0]
        for j in range(PANEL):
            recip.append(1.0 / corner[j][j])
            pivot = jnp.where(row == j, corner[j][j], pivot)
            for i in range(j + 1, PANEL):
                factor[i][j] = corner[i][j] * recip[j]
            for i in range(j + 1, PANEL):
                for m in range(j + 1, i + 1):
                    corner[i][m] = corner[i][m] - factor[i][j] * corner[m][j]
        pivots.append(pivot)
        for j in range(PANEL):
            for m in range(j + 1, PANEL):
                up_rows[m] = up_rows[m] - factor[m][j] * up_rows[j]
                inv_rows[m] = inv_rows[m] - factor[m][j] * inv_rows[j]
        for t in range(p, tiles):
            left = []
            for j in range(PANEL):
                column = columns[j][t]
                for m in range(j):
                    column = column - left[m] * corner[j][m]
                left.append(column * recip[j])
            if t == p:
                left = [jnp.where(row > j, left[j], 0.0) for j in range(PANEL)]
            for j in range(PANEL):
                upper[t] = upper[t] - left[j] * up_rows[j]
                inverse[t] = inverse[t] - left[j] * inv_rows[j]
    scale = [lax.rsqrt(pivot) for pivot in pivots]
    upper = jnp.concatenate([a * b for a, b in zip(upper, scale)], axis=0)
    inverse = jnp.concatenate([a * b for a, b in zip(inverse, scale)], axis=0)
    rid = lax.broadcasted_iota(jnp.int32, (width, width), 0)
    cid = lax.broadcasted_iota(jnp.int32, (width, width), 1)
    lower_t = jnp.where(cid >= rid, upper[:, width:], 0.0)
    rfactor = dot_nt(lower_t, inverse[:, :width])
    rfactor_ref[...] = jnp.where(cid >= rid, rfactor, 0.0)
    solve = inverse[:, width:] * root_scale
    for i in range(mixed_ref.shape[0]):
        basis_ref[:, i * 128:(i + 1) * 128] = jnp.dot(
            solve, mixed_ref[i], precision=HIGHEST, preferred_element_type=F32
        )


def finish(gram, mixed, root_scale):
    blocks, width, lanes = mixed.shape
    return pl.pallas_call(
        functools.partial(finish_kernel, root_scale),
        out_shape=(
            jax.ShapeDtypeStruct((width, blocks * lanes), F32),
            jax.ShapeDtypeStruct((width, width), F32),
        ),
        in_specs=[vmem(), vmem()],
        out_specs=(vmem(), vmem()),
        compiler_params=pltpu.CompilerParams(vmem_limit_bytes=16 * MIB),
        name="finish",
    )(gram, mixed)


def per_device(start_block, weights, neighbours, boundary):
    points = start_block.shape[1]
    blocks, slots, size, _ = weights.shape
    devices = lax.axis_size("tx") * lax.axis_size("ty") * lax.axis_size("tz")
    root_scale = float(points * devices) ** 0.5
    tiles = hold_weights(weights.reshape(blocks, slots * size, size))
    far = halo(take_edges(boundary, start_block))
    mixed, split, edge, keep = first_step(neighbours, boundary, start_block, tiles, far)
    far = halo(edge)
    gram = local_gram(mixed)
    mixed, both = second_step(neighbours, mixed, split, keep, tiles, gram, far)
    return finish(sum_over_devices(both), mixed, root_scale)


def solution(mesh):
    placed = (
        P(None, ("tx", "ty", "tz")),
        P(("tx", "ty", "tz"), None, None, None),
        P(("tx", "ty", "tz"), None),
        P(("tx", "ty", "tz")),
    )
    return jax.shard_map(
        per_device,
        mesh=mesh,
        in_specs=placed,
        out_specs=(P(None, ("tx", "ty", "tz")), P()),
        check_vma=False,
    )
```

```python
import functools

import jax
import jax.numpy as jnp
from jax import lax
from jax.experimental import pallas as pl
from jax.experimental.pallas import tpu as pltpu
from jax.sharding import PartitionSpec as P

F32 = jnp.float32
BF16 = jnp.bfloat16
HIGHEST = lax.Precision.HIGHEST
PLANE = ("tx", "tz")
MIB = 1 << 20
PANEL = 8


def vmem():
    return pl.BlockSpec(memory_space=pltpu.VMEM)


def smem():
    return pl.BlockSpec(memory_space=pltpu.SMEM)


def anywhere():
    return pl.BlockSpec(memory_space=pl.ANY)


def in_hbm(array):
    return pltpu.with_memory_space_constraint(array, pltpu.HBM)


def dot_nt(a, b):
    return lax.dot_general(
        a, b, (((1,), (1,)), ((), ())), precision=HIGHEST, preferred_element_type=F32
    )


def edge_kernel(list_ref, x_ref, edge_ref, bnd_ref, held, list_sem, sem):
    count = edge_ref.shape[0]
    listing = pltpu.make_async_copy(list_ref, bnd_ref, list_sem)
    listing.start()
    listing.wait()
    copies = []
    for j in range(count):
        start = pl.multiple_of(bnd_ref[j] * 128, 128)
        copies.append(
            pltpu.make_async_copy(x_ref.at[:, pl.ds(start, 128)], held.at[j], sem.at[j])
        )
        copies[-1].start()
    for j in range(count):
        copies[j].wait()
        edge_ref[j] = held[j].astype(BF16)


def take_edges(boundary, start_block):
    count = boundary.shape[0]
    width = start_block.shape[0]
    return pl.pallas_call(
        edge_kernel,
        out_shape=jax.ShapeDtypeStruct((count, width, 128), BF16),
        in_specs=[anywhere(), anywhere()],
        out_specs=vmem(),
        scratch_shapes=[
            pltpu.SMEM((count,), jnp.int32),
            pltpu.VMEM((count, width, 128), F32),
            pltpu.SemaphoreType.DMA,
            pltpu.SemaphoreType.DMA((count,)),
        ],
        compiler_params=pltpu.CompilerParams(vmem_limit_bytes=2 * MIB),
        name="edges",
    )(in_hbm(boundary), in_hbm(start_block))


def hold_kernel(w_ref, held_ref, keep_ref, sem):
    copy = pltpu.make_async_copy(w_ref, held_ref, sem)
    copy.start()
    copy.wait()
    ones = jnp.ones((16, w_ref.shape[1]), BF16)
    for i in range(w_ref.shape[0]):
        degree = jnp.dot(ones, held_ref[i], preferred_element_type=F32)
        keep_ref[i] = 1.0 - degree[0:8] * 0.125


def hold_weights(tiles):
    return pl.pallas_call(
        hold_kernel,
        out_shape=(
            jax.ShapeDtypeStruct(tiles.shape, tiles.dtype),
            jax.ShapeDtypeStruct((tiles.shape[0], 8, tiles.shape[2]), F32),
        ),
        in_specs=[anywhere()],
        out_specs=(vmem(), vmem()),
        scratch_shapes=[pltpu.SemaphoreType.DMA],
        compiler_params=pltpu.CompilerParams(vmem_limit_bytes=8 * MIB),
        cost_estimate=pl.CostEstimate(
            flops=0, bytes_accessed=4 * tiles.size, transcendentals=0
        ),
        name="hold_weights",
    )(in_hbm(tiles))


def partners_along(block, axis):
    count = lax.axis_size(axis)

    def pairs(first):
        lows = range(first, count - 1, 2)
        return [(i, i + 1) for i in lows] + [(i + 1, i) for i in lows]

    other = lax.ppermute(block, axis, pairs(1))
    return other, lax.ppermute(block, axis, pairs(0))


def near_kernel(own_ref, mid_ref, pool_ref, sem):
    blocks, listed = own_ref.shape[0], mid_ref.shape[0]
    copies = [
        pltpu.make_async_copy(own_ref, pool_ref.at[pl.ds(0, blocks)], sem.at[0]),
        pltpu.make_async_copy(mid_ref, pool_ref.at[pl.ds(blocks, listed)], sem.at[1]),
    ]
    for copy in copies:
        copy.start()
    for copy in copies:
        copy.wait()


def near_pool(own, mid):
    total = own.shape[0] + 3 * mid.shape[0]
    return pl.pallas_call(
        near_kernel,
        out_shape=jax.ShapeDtypeStruct((total, *own.shape[1:]), own.dtype),
        in_specs=[anywhere(), anywhere()],
        out_specs=vmem(),
        scratch_shapes=[pltpu.SemaphoreType.DMA((2,))],
        compiler_params=pltpu.CompilerParams(vmem_limit_bytes=8 * MIB),
        cost_estimate=pl.CostEstimate(
            flops=0, bytes_accessed=4 * (own.size + mid.size), transcendentals=0
        ),
        name="near_pool",
    )(own, mid)


def halo(own, edge):
    block = edge
    for axis in ("tz", "ty"):
        block = jnp.concatenate([block, *partners_along(block, axis)], axis=0)
    other, partner = partners_along(block, "tx")
    return near_pool(own, block), partner, other


def fill_far(pool_ref, far_refs, sem):
    listed = far_refs[0].shape[0]
    base = pool_ref.shape[0] - 2 * listed
    copies = []
    for j, ref in enumerate(far_refs):
        copies.append(
            pltpu.make_async_copy(ref, pool_ref.at[pl.ds(base + j * listed, listed)], sem.at[j])
        )
        copies[-1].start()
    for copy in copies:
        copy.wait()


def pool_index(codes, blocks, listed):
    place = codes - blocks
    offset = place // listed
    index = jnp.zeros_like(codes)
    for axis, step in (("tx", 9), ("ty", 3), ("tz", 1)):
        way = offset // step % 3
        even = lax.axis_index(axis) % 2 == 0
        last = jnp.where(even, 0, 2) if axis == "tx" else jnp.where(even, 2, 0)
        index = index * 3 + jnp.where(way == 1, 0, jnp.where(way == last, 2, 1))
    return jnp.where(codes < blocks, codes, blocks + index * listed + place % listed)


def first_kernel(
    nbr_ref, bnd_ref, x_ref, w_ref, keep_ref, _, partner_ref, other_ref,
    mixed_ref, split_ref, edge_ref, pool_ref, sem,
):
    blocks, slots = nbr_ref.shape
    width = x_ref.shape[0]
    fill_far(pool_ref, (partner_ref, other_ref), sem)
    for i in range(blocks):
        picked = jnp.concatenate([pool_ref[nbr_ref[i, s]] for s in range(slots)], axis=1)
        out = jnp.dot(picked, w_ref[i], preferred_element_type=F32)
        mixed = x_ref[:, i * 128:(i + 1) * 128] * keep_ref[i, 0:1] + out * 0.125
        mixed_ref[i] = mixed
        head = mixed.astype(BF16)
        split_ref[i, 0:width] = head
        split_ref[i, width:2 * width] = (mixed - head.astype(F32)).astype(BF16)
    for j in range(edge_ref.shape[0]):
        edge_ref[j] = split_ref[bnd_ref[j]]


def first_step(index, boundary, start_block, weights, keep, far):
    blocks = index.shape[0]
    width = start_block.shape[0]
    return pl.pallas_call(
        first_kernel,
        out_shape=(
            jax.ShapeDtypeStruct((blocks, width, 128), F32),
            jax.ShapeDtypeStruct((blocks, 2 * width, 128), BF16),
            jax.ShapeDtypeStruct((boundary.shape[0], 2 * width, 128), BF16),
            jax.ShapeDtypeStruct(far[0].shape, BF16),
        ),
        in_specs=[smem(), smem()] + [vmem()] * 4 + [anywhere()] * 2,
        out_specs=(vmem(),) * 4,
        scratch_shapes=[pltpu.SemaphoreType.DMA((2,))],
        input_output_aliases={5: 3},
        compiler_params=pltpu.CompilerParams(vmem_limit_bytes=16 * MIB),
        name="first_step",
    )(index, boundary, start_block, weights, keep, *far)[:3]


def gram_kernel(mixed_ref, gram_ref):
    total = None
    for i in range(mixed_ref.shape[0]):
        part = dot_nt(mixed_ref[i], mixed_ref[i])
        total = part if total is None else total + part
    gram_ref[...] = total


def local_gram(mixed):
    blocks, width, _ = mixed.shape
    return pl.pallas_call(
        gram_kernel,
        out_shape=jax.ShapeDtypeStruct((width, width), F32),
        in_specs=[vmem()],
        out_specs=vmem(),
        compiler_params=pltpu.CompilerParams(vmem_limit_bytes=8 * MIB),
        cost_estimate=pl.CostEstimate(
            flops=12 * blocks * 128 * width * width,
            bytes_accessed=4 * blocks * 128 * width,
            transcendentals=0,
        ),
        name="first_gram",
    )(mixed)


def second_kernel(
    nbr_ref, mixed_ref, keep_ref, w_ref, gram_ref, _, partner_ref, other_ref,
    out_ref, both_ref, pool_ref, wide, sem,
):
    blocks, slots = nbr_ref.shape
    width = mixed_ref.shape[1]
    fill_far(pool_ref, (partner_ref, other_ref), sem)
    for i in range(blocks):
        picked = jnp.concatenate([pool_ref[nbr_ref[i, s]] for s in range(slots)], axis=1)
        out = jnp.dot(picked, w_ref[i], preferred_element_type=F32)
        mixed = mixed_ref[i] * keep_ref[i, 0:1] + (out[:width] + out[width:]) * 0.125
        out_ref[i] = mixed
        wide[:, i * 128:(i + 1) * 128] = mixed
    both_ref[...] = jnp.concatenate([gram_ref[...], dot_nt(wide[...], wide[...])], axis=1)


def second_step(index, mixed, keep, weights, gram, far):
    blocks = index.shape[0]
    width = mixed.shape[1]
    return pl.pallas_call(
        second_kernel,
        out_shape=(
            jax.ShapeDtypeStruct((blocks, width, 128), F32),
            jax.ShapeDtypeStruct((width, 2 * width), F32),
            jax.ShapeDtypeStruct(far[0].shape, BF16),
        ),
        in_specs=[smem()] + [vmem()] * 5 + [anywhere()] * 2,
        out_specs=(vmem(),) * 3,
        scratch_shapes=[
            pltpu.VMEM((width, blocks * 128), F32),
            pltpu.SemaphoreType.DMA((2,)),
        ],
        input_output_aliases={5: 2},
        compiler_params=pltpu.CompilerParams(vmem_limit_bytes=16 * MIB),
        name="second_step",
    )(index, mixed, keep, weights, gram, *far)[:2]


def sum_over_devices(values):
    rows, lanes = values.shape
    plane = lax.axis_size("tx") * lax.axis_size("tz")
    line = lax.axis_size("ty")
    piece = rows // plane
    parts = lax.all_to_all(values.reshape(plane, piece, lanes), PLANE, 0, 0)
    mine = jnp.sum(parts, axis=0)
    parts = lax.all_to_all(jnp.broadcast_to(mine[None], (line, piece, lanes)), "ty", 0, 0)
    mine = jnp.sum(parts, axis=0)
    parts = lax.all_to_all(jnp.broadcast_to(mine[None], (plane, piece, lanes)), PLANE, 0, 0)
    return parts.reshape(rows, lanes)


def finish_kernel(root_scale, gram_ref, mixed_ref, basis_ref, rfactor_ref):
    width, lanes = gram_ref.shape
    tiles = width // PANEL
    lane = lax.broadcasted_iota(jnp.int32, (PANEL, lanes), 1)
    row = lax.broadcasted_iota(jnp.int32, (PANEL, lanes), 0)
    first = lane < width
    own = jnp.where(first, lane, lane - width)
    upper = [gram_ref[t * PANEL:(t + 1) * PANEL, :] for t in range(tiles)]
    inverse = [(own == row + t * PANEL).astype(F32) for t in range(tiles)]
    pivots = []

    def spread_row(tile, r):
        return jnp.broadcast_to(tile[r:r + 1], tile.shape)

    for p in range(tiles):
        columns = []
        for j in range(PANEL):
            lane_of = jnp.where(first, 0, width) + (p * PANEL + j)
            columns.append([
                jnp.take_along_axis(upper[t], lane_of, axis=1, mode="promise_in_bounds")
                if t >= p else None
                for t in range(tiles)
            ])
        corner = [[spread_row(columns[j][p], i) for j in range(i + 1)] for i in range(PANEL)]
        up_rows = [spread_row(upper[p], j) for j in range(PANEL)]
        inv_rows = [spread_row(inverse[p], j) for j in range(PANEL)]
        factor = [[None] * PANEL for _ in range(PANEL)]
        recip = []
        pivot = corner[0][0]
        for j in range(PANEL):
            recip.append(1.0 / corner[j][j])
            pivot = jnp.where(row == j, corner[j][j], pivot)
            for i in range(j + 1, PANEL):
                factor[i][j] = corner[i][j] * recip[j]
            for i in range(j + 1, PANEL):
                for m in range(j + 1, i + 1):
                    corner[i][m] = corner[i][m] - factor[i][j] * corner[m][j]
        pivots.append(pivot)
        for j in range(PANEL):
            for m in range(j + 1, PANEL):
                up_rows[m] = up_rows[m] - factor[m][j] * up_rows[j]
                inv_rows[m] = inv_rows[m] - factor[m][j] * inv_rows[j]
        for t in range(p, tiles):
            left = []
            for j in range(PANEL):
                column = columns[j][t]
                for m in range(j):
                    column = column - left[m] * corner[j][m]
                left.append(column * recip[j])
            if t == p:
                left = [jnp.where(row > j, left[j], 0.0) for j in range(PANEL)]
            for j in range(PANEL):
                upper[t] = upper[t] - left[j] * up_rows[j]
                inverse[t] = inverse[t] - left[j] * inv_rows[j]
    scale = [lax.rsqrt(pivot) for pivot in pivots]
    upper = jnp.concatenate([a * b for a, b in zip(upper, scale)], axis=0)
    inverse = jnp.concatenate([a * b for a, b in zip(inverse, scale)], axis=0)
    rid = lax.broadcasted_iota(jnp.int32, (width, width), 0)
    cid = lax.broadcasted_iota(jnp.int32, (width, width), 1)
    lower_t = jnp.where(cid >= rid, upper[:, width:], 0.0)
    rfactor = dot_nt(lower_t, inverse[:, :width])
    rfactor_ref[...] = jnp.where(cid >= rid, rfactor, 0.0)
    solve = inverse[:, width:] * root_scale
    for i in range(mixed_ref.shape[0]):
        basis_ref[:, i * 128:(i + 1) * 128] = jnp.dot(
            solve, mixed_ref[i], precision=HIGHEST, preferred_element_type=F32
        )


def finish(gram, mixed, root_scale):
    blocks, width, lanes = mixed.shape
    return pl.pallas_call(
        functools.partial(finish_kernel, root_scale),
        out_shape=(
            jax.ShapeDtypeStruct((width, blocks * lanes), F32),
            jax.ShapeDtypeStruct((width, width), F32),
        ),
        in_specs=[vmem(), vmem()],
        out_specs=(vmem(), vmem()),
        compiler_params=pltpu.CompilerParams(vmem_limit_bytes=16 * MIB),
        name="finish",
    )(gram, mixed)


def per_device(start_block, weights, neighbours, boundary):
    points = start_block.shape[1]
    blocks, slots, size, _ = weights.shape
    devices = lax.axis_size("tx") * lax.axis_size("ty") * lax.axis_size("tz")
    root_scale = float(points * devices) ** 0.5
    tiles, keep = hold_weights(weights.reshape(blocks, slots * size, size))
    index = pool_index(neighbours, blocks, boundary.shape[0])
    own = jnp.swapaxes(start_block.reshape(-1, blocks, size), 0, 1).astype(BF16)
    far = halo(own, take_edges(boundary, start_block))
    mixed, split, edge = first_step(index, boundary, start_block, tiles, keep, far)
    far = halo(split, edge)
    gram = local_gram(mixed)
    mixed, both = second_step(index, mixed, keep, tiles, gram, far)
    return finish(sum_over_devices(both), mixed, root_scale)


def solution(mesh):
    placed = (
        P(None, ("tx", "ty", "tz")),
        P(("tx", "ty", "tz"), None, None, None),
        P(("tx", "ty", "tz"), None),
        P(("tx", "ty", "tz")),
    )
    return jax.shard_map(
        per_device,
        mesh=mesh,
        in_specs=placed,
        out_specs=(P(None, ("tx", "ty", "tz")), P()),
        check_vma=False,
    )
```

```python
import functools

import jax
import jax.numpy as jnp
from jax import lax
from jax.experimental import pallas as pl
from jax.experimental.pallas import tpu as pltpu
from jax.sharding import PartitionSpec as P

F32 = jnp.float32
BF16 = jnp.bfloat16
HIGHEST = lax.Precision.HIGHEST
PLANE = ("tx", "tz")
MIB = 1 << 20
PANEL = 8
SHARE = 0.875


def vmem():
    return pl.BlockSpec(memory_space=pltpu.VMEM)


def smem():
    return pl.BlockSpec(memory_space=pltpu.SMEM)


def anywhere():
    return pl.BlockSpec(memory_space=pl.ANY)


def in_hbm(array):
    return pltpu.with_memory_space_constraint(array, pltpu.HBM)


def dot_nt(a, b):
    return lax.dot_general(
        a, b, (((1,), (1,)), ((), ())), precision=HIGHEST, preferred_element_type=F32
    )


def edge_kernel(list_ref, x_ref, edge_ref, bnd_ref, held, list_sem, sem):
    count = edge_ref.shape[0]
    listing = pltpu.make_async_copy(list_ref, bnd_ref, list_sem)
    listing.start()
    listing.wait()
    copies = []
    for j in range(count):
        start = pl.multiple_of(bnd_ref[j] * 128, 128)
        copies.append(
            pltpu.make_async_copy(x_ref.at[:, pl.ds(start, 128)], held.at[j], sem.at[j])
        )
        copies[-1].start()
    for j in range(count):
        copies[j].wait()
        edge_ref[j] = held[j].astype(BF16)


def take_edges(boundary, start_block):
    count = boundary.shape[0]
    width = start_block.shape[0]
    return pl.pallas_call(
        edge_kernel,
        out_shape=jax.ShapeDtypeStruct((count, width, 128), BF16),
        in_specs=[anywhere(), anywhere()],
        out_specs=vmem(),
        scratch_shapes=[
            pltpu.SMEM((count,), jnp.int32),
            pltpu.VMEM((count, width, 128), F32),
            pltpu.SemaphoreType.DMA,
            pltpu.SemaphoreType.DMA((count,)),
        ],
        compiler_params=pltpu.CompilerParams(vmem_limit_bytes=2 * MIB),
        name="edges",
    )(in_hbm(boundary), in_hbm(start_block))


def hold_kernel(w_ref, held_ref, keep_ref, sem):
    copy = pltpu.make_async_copy(w_ref, held_ref, sem)
    copy.start()
    copy.wait()
    ones = jnp.ones((16, w_ref.shape[1]), BF16)
    for i in range(w_ref.shape[0]):
        degree = jnp.dot(ones, held_ref[i], preferred_element_type=F32)
        keep_ref[i] = 1.0 - degree[0:8] * 0.125


def hold_weights(tiles):
    return pl.pallas_call(
        hold_kernel,
        out_shape=(
            jax.ShapeDtypeStruct(tiles.shape, tiles.dtype),
            jax.ShapeDtypeStruct((tiles.shape[0], 8, tiles.shape[2]), F32),
        ),
        in_specs=[anywhere()],
        out_specs=(vmem(), vmem()),
        scratch_shapes=[pltpu.SemaphoreType.DMA],
        compiler_params=pltpu.CompilerParams(vmem_limit_bytes=8 * MIB),
        cost_estimate=pl.CostEstimate(
            flops=0, bytes_accessed=4 * tiles.size, transcendentals=0
        ),
        name="hold_weights",
    )(in_hbm(tiles))


def partners_along(block, axis):
    count = lax.axis_size(axis)

    def pairs(first):
        lows = range(first, count - 1, 2)
        return [(i, i + 1) for i in lows] + [(i + 1, i) for i in lows]

    other = lax.ppermute(block, axis, pairs(1))
    return other, lax.ppermute(block, axis, pairs(0))


def near_kernel(own_ref, mid_ref, pool_ref, sem):
    blocks, listed = own_ref.shape[0], mid_ref.shape[0]
    copies = [
        pltpu.make_async_copy(own_ref, pool_ref.at[pl.ds(0, blocks)], sem.at[0]),
        pltpu.make_async_copy(mid_ref, pool_ref.at[pl.ds(blocks, listed)], sem.at[1]),
    ]
    for copy in copies:
        copy.start()
    for copy in copies:
        copy.wait()


def near_pool(own, mid):
    total = own.shape[0] + 3 * mid.shape[0]
    return pl.pallas_call(
        near_kernel,
        out_shape=jax.ShapeDtypeStruct((total, *own.shape[1:]), own.dtype),
        in_specs=[anywhere(), anywhere()],
        out_specs=vmem(),
        scratch_shapes=[pltpu.SemaphoreType.DMA((2,))],
        compiler_params=pltpu.CompilerParams(vmem_limit_bytes=8 * MIB),
        cost_estimate=pl.CostEstimate(
            flops=0, bytes_accessed=4 * (own.size + mid.size), transcendentals=0
        ),
        name="near_pool",
    )(own, mid)


def halo(own, edge):
    block = edge
    for axis in ("tz", "ty"):
        block = jnp.concatenate([block, *partners_along(block, axis)], axis=0)
    other, partner = partners_along(block, "tx")
    return near_pool(own, block), partner, other


def fill_far(pool_ref, far_refs, sem):
    listed = far_refs[0].shape[0]
    base = pool_ref.shape[0] - 2 * listed
    copies = []
    for j, ref in enumerate(far_refs):
        copies.append(
            pltpu.make_async_copy(ref, pool_ref.at[pl.ds(base + j * listed, listed)], sem.at[j])
        )
        copies[-1].start()
    for copy in copies:
        copy.wait()


def pool_index(codes, blocks, listed):
    place = codes - blocks
    offset = place // listed
    index = jnp.zeros_like(codes)
    for axis, step in (("tx", 9), ("ty", 3), ("tz", 1)):
        way = offset // step % 3
        even = lax.axis_index(axis) % 2 == 0
        last = jnp.where(even, 0, 2) if axis == "tx" else jnp.where(even, 2, 0)
        index = index * 3 + jnp.where(way == 1, 0, jnp.where(way == last, 2, 1))
    return jnp.where(codes < blocks, codes, blocks + index * listed + place % listed)


def first_kernel(
    nbr_ref, bnd_ref, x_ref, w_ref, keep_ref, _, partner_ref, other_ref,
    mixed_ref, base_ref, step_ref, edge_ref, pool_ref, sem,
):
    blocks, slots = nbr_ref.shape
    fill_far(pool_ref, (partner_ref, other_ref), sem)
    for i in range(blocks):
        picked = jnp.concatenate([pool_ref[nbr_ref[i, s]] for s in range(slots)], axis=1)
        out = jnp.dot(picked, w_ref[i], preferred_element_type=F32) * 0.125
        keep = keep_ref[i, 0:1]
        mixed = x_ref[:, i * 128:(i + 1) * 128] * keep + out
        mixed_ref[i] = mixed
        base_ref[i] = mixed * keep + out * SHARE
        step_ref[i] = (mixed - pool_ref[i].astype(F32) * SHARE).astype(BF16)
    for j in range(edge_ref.shape[0]):
        edge_ref[j] = step_ref[bnd_ref[j]]


def first_step(index, boundary, start_block, weights, keep, far):
    blocks = index.shape[0]
    width = start_block.shape[0]
    return pl.pallas_call(
        first_kernel,
        out_shape=(
            jax.ShapeDtypeStruct((blocks, width, 128), F32),
            jax.ShapeDtypeStruct((blocks, width, 128), F32),
            jax.ShapeDtypeStruct((blocks, width, 128), BF16),
            jax.ShapeDtypeStruct((boundary.shape[0], width, 128), BF16),
            jax.ShapeDtypeStruct(far[0].shape, BF16),
        ),
        in_specs=[smem(), smem()] + [vmem()] * 4 + [anywhere()] * 2,
        out_specs=(vmem(),) * 5,
        scratch_shapes=[pltpu.SemaphoreType.DMA((2,))],
        input_output_aliases={5: 4},
        compiler_params=pltpu.CompilerParams(vmem_limit_bytes=16 * MIB),
        name="first_step",
    )(index, boundary, start_block, weights, keep, *far)[:4]


def gram_kernel(mixed_ref, gram_ref):
    total = None
    for i in range(mixed_ref.shape[0]):
        part = dot_nt(mixed_ref[i], mixed_ref[i])
        total = part if total is None else total + part
    gram_ref[...] = total


def local_gram(mixed):
    blocks, width, _ = mixed.shape
    return pl.pallas_call(
        gram_kernel,
        out_shape=jax.ShapeDtypeStruct((width, width), F32),
        in_specs=[vmem()],
        out_specs=vmem(),
        compiler_params=pltpu.CompilerParams(vmem_limit_bytes=8 * MIB),
        cost_estimate=pl.CostEstimate(
            flops=12 * blocks * 128 * width * width,
            bytes_accessed=4 * blocks * 128 * width,
            transcendentals=0,
        ),
        name="first_gram",
    )(mixed)


def second_kernel(
    nbr_ref, base_ref, w_ref, gram_ref, _, partner_ref, other_ref,
    out_ref, both_ref, pool_ref, wide, sem,
):
    blocks, slots = nbr_ref.shape
    fill_far(pool_ref, (partner_ref, other_ref), sem)
    for i in range(blocks):
        picked = jnp.concatenate([pool_ref[nbr_ref[i, s]] for s in range(slots)], axis=1)
        out = jnp.dot(picked, w_ref[i], preferred_element_type=F32)
        mixed = base_ref[i] + out * 0.125
        out_ref[i] = mixed
        wide[:, i * 128:(i + 1) * 128] = mixed
    both_ref[...] = jnp.concatenate([gram_ref[...], dot_nt(wide[...], wide[...])], axis=1)


def second_step(index, base, weights, gram, far):
    blocks, width, _ = base.shape
    return pl.pallas_call(
        second_kernel,
        out_shape=(
            jax.ShapeDtypeStruct((blocks, width, 128), F32),
            jax.ShapeDtypeStruct((width, 2 * width), F32),
            jax.ShapeDtypeStruct(far[0].shape, BF16),
        ),
        in_specs=[smem()] + [vmem()] * 4 + [anywhere()] * 2,
        out_specs=(vmem(),) * 3,
        scratch_shapes=[
            pltpu.VMEM((width, blocks * 128), F32),
            pltpu.SemaphoreType.DMA((2,)),
        ],
        input_output_aliases={4: 2},
        compiler_params=pltpu.CompilerParams(vmem_limit_bytes=16 * MIB),
        name="second_step",
    )(index, base, weights, gram, *far)[:2]


def sum_over_devices(values):
    rows, lanes = values.shape
    plane = lax.axis_size("tx") * lax.axis_size("tz")
    line = lax.axis_size("ty")
    piece = rows // plane
    parts = lax.all_to_all(values.reshape(plane, piece, lanes), PLANE, 0, 0)
    mine = jnp.sum(parts, axis=0)
    parts = lax.all_to_all(jnp.broadcast_to(mine[None], (line, piece, lanes)), "ty", 0, 0)
    mine = jnp.sum(parts, axis=0)
    parts = lax.all_to_all(jnp.broadcast_to(mine[None], (plane, piece, lanes)), PLANE, 0, 0)
    return parts.reshape(rows, lanes)


def finish_kernel(root_scale, gram_ref, mixed_ref, basis_ref, rfactor_ref):
    width, lanes = gram_ref.shape
    tiles = width // PANEL
    lane = lax.broadcasted_iota(jnp.int32, (PANEL, lanes), 1)
    row = lax.broadcasted_iota(jnp.int32, (PANEL, lanes), 0)
    first = lane < width
    own = jnp.where(first, lane, lane - width)
    upper = [gram_ref[t * PANEL:(t + 1) * PANEL, :] for t in range(tiles)]
    inverse = [(own == row + t * PANEL).astype(F32) for t in range(tiles)]
    pivots = []

    def spread_row(tile, r):
        return jnp.broadcast_to(tile[r:r + 1], tile.shape)

    for p in range(tiles):
        columns = []
        for j in range(PANEL):
            lane_of = jnp.where(first, 0, width) + (p * PANEL + j)
            columns.append([
                jnp.take_along_axis(upper[t], lane_of, axis=1, mode="promise_in_bounds")
                if t >= p else None
                for t in range(tiles)
            ])
        corner = [[spread_row(columns[j][p], i) for j in range(i + 1)] for i in range(PANEL)]
        up_rows = [spread_row(upper[p], j) for j in range(PANEL)]
        inv_rows = [spread_row(inverse[p], j) for j in range(PANEL)]
        factor = [[None] * PANEL for _ in range(PANEL)]
        recip = []
        pivot = corner[0][0]
        for j in range(PANEL):
            recip.append(1.0 / corner[j][j])
            pivot = jnp.where(row == j, corner[j][j], pivot)
            for i in range(j + 1, PANEL):
                factor[i][j] = corner[i][j] * recip[j]
            for i in range(j + 1, PANEL):
                for m in range(j + 1, i + 1):
                    corner[i][m] = corner[i][m] - factor[i][j] * corner[m][j]
        pivots.append(pivot)
        for j in range(PANEL):
            for m in range(j + 1, PANEL):
                up_rows[m] = up_rows[m] - factor[m][j] * up_rows[j]
                inv_rows[m] = inv_rows[m] - factor[m][j] * inv_rows[j]
        for t in range(p, tiles):
            left = []
            for j in range(PANEL):
                column = columns[j][t]
                for m in range(j):
                    column = column - left[m] * corner[j][m]
                left.append(column * recip[j])
            if t == p:
                left = [jnp.where(row > j, left[j], 0.0) for j in range(PANEL)]
            for j in range(PANEL):
                upper[t] = upper[t] - left[j] * up_rows[j]
                inverse[t] = inverse[t] - left[j] * inv_rows[j]
    scale = [lax.rsqrt(pivot) for pivot in pivots]
    upper = jnp.concatenate([a * b for a, b in zip(upper, scale)], axis=0)
    inverse = jnp.concatenate([a * b for a, b in zip(inverse, scale)], axis=0)
    rid = lax.broadcasted_iota(jnp.int32, (width, width), 0)
    cid = lax.broadcasted_iota(jnp.int32, (width, width), 1)
    lower_t = jnp.where(cid >= rid, upper[:, width:], 0.0)
    rfactor = dot_nt(lower_t, inverse[:, :width])
    rfactor_ref[...] = jnp.where(cid >= rid, rfactor, 0.0)
    solve = inverse[:, width:] * root_scale
    for i in range(mixed_ref.shape[0]):
        basis_ref[:, i * 128:(i + 1) * 128] = jnp.dot(
            solve, mixed_ref[i], precision=HIGHEST, preferred_element_type=F32
        )


def finish(gram, mixed, root_scale):
    blocks, width, lanes = mixed.shape
    return pl.pallas_call(
        functools.partial(finish_kernel, root_scale),
        out_shape=(
            jax.ShapeDtypeStruct((width, blocks * lanes), F32),
            jax.ShapeDtypeStruct((width, width), F32),
        ),
        in_specs=[vmem(), vmem()],
        out_specs=(vmem(), vmem()),
        compiler_params=pltpu.CompilerParams(vmem_limit_bytes=16 * MIB),
        name="finish",
    )(gram, mixed)


def per_device(start_block, weights, neighbours, boundary):
    points = start_block.shape[1]
    blocks, slots, size, _ = weights.shape
    devices = lax.axis_size("tx") * lax.axis_size("ty") * lax.axis_size("tz")
    root_scale = float(points * devices) ** 0.5
    tiles, keep = hold_weights(weights.reshape(blocks, slots * size, size))
    index = pool_index(neighbours, blocks, boundary.shape[0])
    own = jnp.swapaxes(start_block.reshape(-1, blocks, size), 0, 1).astype(BF16)
    far = halo(own, take_edges(boundary, start_block))
    mixed, base, step, edge = first_step(index, boundary, start_block, tiles, keep, far)
    far = halo(step, edge)
    gram = local_gram(mixed)
    mixed, both = second_step(index, base, tiles, gram, far)
    return finish(sum_over_devices(both), mixed, root_scale)


def solution(mesh):
    placed = (
        P(None, ("tx", "ty", "tz")),
        P(("tx", "ty", "tz"), None, None, None),
        P(("tx", "ty", "tz"), None),
        P(("tx", "ty", "tz")),
    )
    return jax.shard_map(
        per_device,
        mesh=mesh,
        in_specs=placed,
        out_specs=(P(None, ("tx", "ty", "tz")), P()),
        check_vma=False,
    )
```

```python
import functools

import jax
import jax.numpy as jnp
from jax import lax
from jax.experimental import pallas as pl
from jax.experimental.pallas import tpu as pltpu
from jax.sharding import PartitionSpec as P

F32 = jnp.float32
BF16 = jnp.bfloat16
HIGHEST = lax.Precision.HIGHEST
PLANE = ("tx", "tz")
MIB = 1 << 20
PANEL = 8
SHARE = 0.875


def vmem():
    return pl.BlockSpec(memory_space=pltpu.VMEM)


def smem():
    return pl.BlockSpec(memory_space=pltpu.SMEM)


def anywhere():
    return pl.BlockSpec(memory_space=pl.ANY)


def in_hbm(array):
    return pltpu.with_memory_space_constraint(array, pltpu.HBM)


def dot_nt(a, b):
    return lax.dot_general(
        a, b, (((1,), (1,)), ((), ())), precision=HIGHEST, preferred_element_type=F32
    )


def edge_kernel(list_ref, x_ref, edge_ref, bnd_ref, held, sem):
    copies = [
        pltpu.make_async_copy(list_ref, bnd_ref, sem.at[0]),
        pltpu.make_async_copy(x_ref, held, sem.at[1]),
    ]
    for copy in copies:
        copy.start()
    for copy in copies:
        copy.wait()
    for j in range(edge_ref.shape[0]):
        start = pl.multiple_of(bnd_ref[j] * 128, 128)
        edge_ref[j] = held[:, pl.ds(start, 128)].astype(BF16)


def take_edges(boundary, start_block):
    count = boundary.shape[0]
    width = start_block.shape[0]
    return pl.pallas_call(
        edge_kernel,
        out_shape=jax.ShapeDtypeStruct((count, width, 128), BF16),
        in_specs=[anywhere(), anywhere()],
        out_specs=vmem(),
        scratch_shapes=[
            pltpu.SMEM((count,), jnp.int32),
            pltpu.VMEM(start_block.shape, F32),
            pltpu.SemaphoreType.DMA((2,)),
        ],
        compiler_params=pltpu.CompilerParams(vmem_limit_bytes=2 * MIB),
        name="edges",
    )(in_hbm(boundary), in_hbm(start_block))


def hold_kernel(w_ref, held_ref, keep_ref, sem):
    copy = pltpu.make_async_copy(w_ref, held_ref, sem)
    copy.start()
    copy.wait()
    ones = jnp.ones((16, w_ref.shape[1]), BF16)
    for i in range(w_ref.shape[0]):
        degree = jnp.dot(ones, held_ref[i], preferred_element_type=F32)
        keep_ref[i] = 1.0 - degree[0:8] * 0.125


def hold_weights(tiles):
    return pl.pallas_call(
        hold_kernel,
        out_shape=(
            jax.ShapeDtypeStruct(tiles.shape, tiles.dtype),
            jax.ShapeDtypeStruct((tiles.shape[0], 8, tiles.shape[2]), F32),
        ),
        in_specs=[anywhere()],
        out_specs=(vmem(), vmem()),
        scratch_shapes=[pltpu.SemaphoreType.DMA],
        compiler_params=pltpu.CompilerParams(vmem_limit_bytes=8 * MIB),
        cost_estimate=pl.CostEstimate(
            flops=0, bytes_accessed=4 * tiles.size, transcendentals=0
        ),
        name="hold_weights",
    )(in_hbm(tiles))


def partners_along(block, axis):
    count = lax.axis_size(axis)

    def pairs(first):
        lows = range(first, count - 1, 2)
        return [(i, i + 1) for i in lows] + [(i + 1, i) for i in lows]

    other = lax.ppermute(block, axis, pairs(1))
    return other, lax.ppermute(block, axis, pairs(0))


def near_kernel(own_ref, mid_ref, pool_ref, sem):
    blocks, listed = own_ref.shape[0], mid_ref.shape[0]
    copies = [
        pltpu.make_async_copy(own_ref, pool_ref.at[pl.ds(0, blocks)], sem.at[0]),
        pltpu.make_async_copy(mid_ref, pool_ref.at[pl.ds(blocks, listed)], sem.at[1]),
    ]
    for copy in copies:
        copy.start()
    for copy in copies:
        copy.wait()


def near_pool(own, mid):
    total = own.shape[0] + 3 * mid.shape[0]
    return pl.pallas_call(
        near_kernel,
        out_shape=jax.ShapeDtypeStruct((total, *own.shape[1:]), own.dtype),
        in_specs=[anywhere(), anywhere()],
        out_specs=vmem(),
        scratch_shapes=[pltpu.SemaphoreType.DMA((2,))],
        compiler_params=pltpu.CompilerParams(vmem_limit_bytes=8 * MIB),
        cost_estimate=pl.CostEstimate(
            flops=0, bytes_accessed=4 * (own.size + mid.size), transcendentals=0
        ),
        name="near_pool",
    )(own, mid)


def halo(own, edge):
    block = edge
    for axis in ("tz", "ty"):
        block = jnp.concatenate([block, *partners_along(block, axis)], axis=0)
    other, partner = partners_along(block, "tx")
    return near_pool(own, block), partner, other


def fill_far(pool_ref, far_refs, sem):
    listed = far_refs[0].shape[0]
    base = pool_ref.shape[0] - 2 * listed
    copies = []
    for j, ref in enumerate(far_refs):
        copies.append(
            pltpu.make_async_copy(ref, pool_ref.at[pl.ds(base + j * listed, listed)], sem.at[j])
        )
        copies[-1].start()
    for copy in copies:
        copy.wait()


def pool_index(codes, blocks, listed):
    place = codes - blocks
    offset = place // listed
    index = jnp.zeros_like(codes)
    for axis, step in (("tx", 9), ("ty", 3), ("tz", 1)):
        way = offset // step % 3
        even = lax.axis_index(axis) % 2 == 0
        last = jnp.where(even, 0, 2) if axis == "tx" else jnp.where(even, 2, 0)
        index = index * 3 + jnp.where(way == 1, 0, jnp.where(way == last, 2, 1))
    return jnp.where(codes < blocks, codes, blocks + index * listed + place % listed)


def gather_sum(table_ref, pool_ref, w_ref, slots, i):
    picked = [pool_ref[table_ref[i * slots + s]] for s in range(slots)]
    return jnp.dot(jnp.concatenate(picked, axis=1), w_ref[i], preferred_element_type=F32)


def first_row(slots, table_ref, x_ref, w_ref, keep_ref, pool_ref, i, lanes):
    out = gather_sum(table_ref, pool_ref, w_ref, slots, i) * 0.125
    keep = keep_ref[i, 0:1]
    mixed = x_ref[:, lanes] * keep + out
    step = (mixed - pool_ref[i].astype(F32) * SHARE).astype(BF16)
    return mixed, mixed * keep + out * SHARE, step


def listed_kernel(
    slots, table_ref, x_ref, w_ref, keep_ref, _, partner_ref, other_ref,
    edge_ref, pool_ref, sem,
):
    fill_far(pool_ref, (partner_ref, other_ref), sem)
    first = w_ref.shape[0] * slots
    for j in range(edge_ref.shape[0]):
        i = table_ref[first + j]
        lanes = pl.ds(pl.multiple_of(i * 128, 128), 128)
        edge_ref[j] = first_row(slots, table_ref, x_ref, w_ref, keep_ref, pool_ref, i, lanes)[2]


def listed_rows(table, count, start_block, weights, keep, far):
    blocks, depth, size = weights.shape
    width = start_block.shape[0]
    return pl.pallas_call(
        functools.partial(listed_kernel, depth // size),
        out_shape=(
            jax.ShapeDtypeStruct((count, width, size), BF16),
            jax.ShapeDtypeStruct(far[0].shape, BF16),
        ),
        in_specs=[smem()] + [vmem()] * 4 + [anywhere()] * 2,
        out_specs=(vmem(),) * 2,
        scratch_shapes=[pltpu.SemaphoreType.DMA((2,))],
        input_output_aliases={4: 1},
        compiler_params=pltpu.CompilerParams(vmem_limit_bytes=16 * MIB),
        name="listed_rows",
    )(table, start_block, weights, keep, *far)


def first_kernel(
    slots, table_ref, x_ref, w_ref, keep_ref, pool_ref, mixed_ref, base_ref, step_ref
):
    for i in range(w_ref.shape[0]):
        lanes = slice(i * 128, (i + 1) * 128)
        mixed_ref[i], base_ref[i], step_ref[i] = first_row(
            slots, table_ref, x_ref, w_ref, keep_ref, pool_ref, i, lanes
        )


def first_step(table, start_block, weights, keep, pool):
    blocks, depth, size = weights.shape
    width = start_block.shape[0]
    shape = (blocks, width, size)
    return pl.pallas_call(
        functools.partial(first_kernel, depth // size),
        out_shape=(
            jax.ShapeDtypeStruct(shape, F32),
            jax.ShapeDtypeStruct(shape, F32),
            jax.ShapeDtypeStruct(shape, BF16),
        ),
        in_specs=[smem()] + [vmem()] * 4,
        out_specs=(vmem(),) * 3,
        compiler_params=pltpu.CompilerParams(vmem_limit_bytes=16 * MIB),
        cost_estimate=pl.CostEstimate(
            flops=2 * width * blocks * depth * size,
            bytes_accessed=2 * weights.size,
            transcendentals=0,
        ),
        name="first_step",
    )(table, start_block, weights, keep, pool)


def gram_kernel(mixed_ref, gram_ref):
    total = None
    for i in range(mixed_ref.shape[0]):
        part = dot_nt(mixed_ref[i], mixed_ref[i])
        total = part if total is None else total + part
    gram_ref[...] = total


def local_gram(mixed):
    blocks, width, _ = mixed.shape
    return pl.pallas_call(
        gram_kernel,
        out_shape=jax.ShapeDtypeStruct((width, width), F32),
        in_specs=[vmem()],
        out_specs=vmem(),
        compiler_params=pltpu.CompilerParams(vmem_limit_bytes=8 * MIB),
        cost_estimate=pl.CostEstimate(
            flops=12 * blocks * 128 * width * width,
            bytes_accessed=4 * blocks * 128 * width,
            transcendentals=0,
        ),
        name="first_gram",
    )(mixed)


def second_kernel(
    slots, table_ref, base_ref, w_ref, gram_ref, _, partner_ref, other_ref,
    out_ref, both_ref, pool_ref, wide, sem,
):
    fill_far(pool_ref, (partner_ref, other_ref), sem)
    for i in range(w_ref.shape[0]):
        mixed = base_ref[i] + gather_sum(table_ref, pool_ref, w_ref, slots, i) * 0.125
        out_ref[i] = mixed
        wide[:, i * 128:(i + 1) * 128] = mixed
    both_ref[...] = jnp.concatenate([gram_ref[...], dot_nt(wide[...], wide[...])], axis=1)


def second_step(table, base, weights, gram, far):
    blocks, width, _ = base.shape
    return pl.pallas_call(
        functools.partial(second_kernel, weights.shape[1] // weights.shape[2]),
        out_shape=(
            jax.ShapeDtypeStruct((blocks, width, 128), F32),
            jax.ShapeDtypeStruct((width, 2 * width), F32),
            jax.ShapeDtypeStruct(far[0].shape, BF16),
        ),
        in_specs=[smem()] + [vmem()] * 4 + [anywhere()] * 2,
        out_specs=(vmem(),) * 3,
        scratch_shapes=[
            pltpu.VMEM((width, blocks * 128), F32),
            pltpu.SemaphoreType.DMA((2,)),
        ],
        input_output_aliases={4: 2},
        compiler_params=pltpu.CompilerParams(vmem_limit_bytes=16 * MIB),
        name="second_step",
    )(table, base, weights, gram, *far)[:2]


def sum_over_devices(values):
    rows, lanes = values.shape
    plane = lax.axis_size("tx") * lax.axis_size("tz")
    line = lax.axis_size("ty")
    piece = rows // plane
    parts = lax.all_to_all(values.reshape(plane, piece, lanes), PLANE, 0, 0)
    mine = jnp.sum(parts, axis=0)
    parts = lax.all_to_all(jnp.broadcast_to(mine[None], (line, piece, lanes)), "ty", 0, 0)
    mine = jnp.sum(parts, axis=0)
    parts = lax.all_to_all(jnp.broadcast_to(mine[None], (plane, piece, lanes)), PLANE, 0, 0)
    return parts.reshape(rows, lanes)


def finish_kernel(root_scale, gram_ref, mixed_ref, basis_ref, rfactor_ref):
    width, lanes = gram_ref.shape
    tiles = width // PANEL
    lane = lax.broadcasted_iota(jnp.int32, (PANEL, lanes), 1)
    row = lax.broadcasted_iota(jnp.int32, (PANEL, lanes), 0)
    first = lane < width
    own = jnp.where(first, lane, lane - width)
    upper = [gram_ref[t * PANEL:(t + 1) * PANEL, :] for t in range(tiles)]
    inverse = [(own == row + t * PANEL).astype(F32) for t in range(tiles)]
    pivots = []

    def spread_row(tile, r):
        return jnp.broadcast_to(tile[r:r + 1], tile.shape)

    for p in range(tiles):
        columns = []
        for j in range(PANEL):
            lane_of = jnp.where(first, 0, width) + (p * PANEL + j)
            columns.append([
                jnp.take_along_axis(upper[t], lane_of, axis=1, mode="promise_in_bounds")
                if t >= p else None
                for t in range(tiles)
            ])
        corner = [[spread_row(columns[j][p], i) for j in range(i + 1)] for i in range(PANEL)]
        up_rows = [spread_row(upper[p], j) for j in range(PANEL)]
        inv_rows = [spread_row(inverse[p], j) for j in range(PANEL)]
        factor = [[None] * PANEL for _ in range(PANEL)]
        recip = []
        pivot = corner[0][0]
        for j in range(PANEL):
            recip.append(1.0 / corner[j][j])
            pivot = jnp.where(row == j, corner[j][j], pivot)
            for i in range(j + 1, PANEL):
                factor[i][j] = corner[i][j] * recip[j]
            for i in range(j + 1, PANEL):
                for m in range(j + 1, i + 1):
                    corner[i][m] = corner[i][m] - factor[i][j] * corner[m][j]
        pivots.append(pivot)
        for j in range(PANEL):
            for m in range(j + 1, PANEL):
                up_rows[m] = up_rows[m] - factor[m][j] * up_rows[j]
                inv_rows[m] = inv_rows[m] - factor[m][j] * inv_rows[j]
        for t in range(p, tiles):
            left = []
            for j in range(PANEL):
                column = columns[j][t]
                for m in range(j):
                    column = column - left[m] * corner[j][m]
                left.append(column * recip[j])
            if t == p:
                left = [jnp.where(row > j, left[j], 0.0) for j in range(PANEL)]
            for j in range(PANEL):
                upper[t] = upper[t] - left[j] * up_rows[j]
                inverse[t] = inverse[t] - left[j] * inv_rows[j]
    scale = [lax.rsqrt(pivot) for pivot in pivots]
    upper = jnp.concatenate([a * b for a, b in zip(upper, scale)], axis=0)
    inverse = jnp.concatenate([a * b for a, b in zip(inverse, scale)], axis=0)
    rid = lax.broadcasted_iota(jnp.int32, (width, width), 0)
    cid = lax.broadcasted_iota(jnp.int32, (width, width), 1)
    lower_t = jnp.where(cid >= rid, upper[:, width:], 0.0)
    rfactor = dot_nt(lower_t, inverse[:, :width])
    rfactor_ref[...] = jnp.where(cid >= rid, rfactor, 0.0)
    solve = inverse[:, width:] * root_scale
    for i in range(mixed_ref.shape[0]):
        basis_ref[:, i * 128:(i + 1) * 128] = jnp.dot(
            solve, mixed_ref[i], precision=HIGHEST, preferred_element_type=F32
        )


def finish(gram, mixed, root_scale):
    blocks, width, lanes = mixed.shape
    return pl.pallas_call(
        functools.partial(finish_kernel, root_scale),
        out_shape=(
            jax.ShapeDtypeStruct((width, blocks * lanes), F32),
            jax.ShapeDtypeStruct((width, width), F32),
        ),
        in_specs=[vmem(), vmem()],
        out_specs=(vmem(), vmem()),
        compiler_params=pltpu.CompilerParams(vmem_limit_bytes=16 * MIB),
        name="finish",
    )(gram, mixed)


def per_device(start_block, weights, neighbours, boundary):
    points = start_block.shape[1]
    blocks, slots, size, _ = weights.shape
    devices = lax.axis_size("tx") * lax.axis_size("ty") * lax.axis_size("tz")
    root_scale = float(points * devices) ** 0.5
    tiles, keep = hold_weights(weights.reshape(blocks, slots * size, size))
    listed = boundary.shape[0]
    index = pool_index(neighbours, blocks, listed)
    table = jnp.concatenate([index.reshape(-1), boundary])
    own = jnp.swapaxes(start_block.reshape(-1, blocks, size), 0, 1).astype(BF16)
    far = halo(own, take_edges(boundary, start_block))
    edge, pool = listed_rows(table, listed, start_block, tiles, keep, far)
    mixed, base, step = first_step(table, start_block, tiles, keep, pool)
    far = halo(step, edge)
    gram = local_gram(mixed)
    mixed, both = second_step(table, base, tiles, gram, far)
    return finish(sum_over_devices(both), mixed, root_scale)


def solution(mesh):
    placed = (
        P(None, ("tx", "ty", "tz")),
        P(("tx", "ty", "tz"), None, None, None),
        P(("tx", "ty", "tz"), None),
        P(("tx", "ty", "tz")),
    )
    return jax.shard_map(
        per_device,
        mesh=mesh,
        in_specs=placed,
        out_specs=(P(None, ("tx", "ty", "tz")), P()),
        check_vma=False,
    )
```

```python
import functools

import jax
import jax.numpy as jnp
from jax import lax
from jax.experimental import pallas as pl
from jax.experimental.pallas import tpu as pltpu
from jax.sharding import PartitionSpec as P

F32 = jnp.float32
BF16 = jnp.bfloat16
HIGHEST = lax.Precision.HIGHEST
PLANE = ("tx", "tz")
MIB = 1 << 20
PANEL = 8
SHARE = 0.875


def vmem():
    return pl.BlockSpec(memory_space=pltpu.VMEM)


def smem():
    return pl.BlockSpec(memory_space=pltpu.SMEM)


def anywhere():
    return pl.BlockSpec(memory_space=pl.ANY)


def in_hbm(array):
    return pltpu.with_memory_space_constraint(array, pltpu.HBM)


def dot_nt(a, b):
    return lax.dot_general(
        a, b, (((1,), (1,)), ((), ())), precision=HIGHEST, preferred_element_type=F32
    )


def edge_kernel(list_ref, x_ref, edge_ref, bnd_ref, held, sem):
    copies = [
        pltpu.make_async_copy(list_ref, bnd_ref, sem.at[0]),
        pltpu.make_async_copy(x_ref, held, sem.at[1]),
    ]
    for copy in copies:
        copy.start()
    for copy in copies:
        copy.wait()
    for j in range(edge_ref.shape[0]):
        start = pl.multiple_of(bnd_ref[j] * 128, 128)
        edge_ref[j] = held[:, pl.ds(start, 128)].astype(BF16)


def take_edges(boundary, start_block):
    count = boundary.shape[0]
    width = start_block.shape[0]
    return pl.pallas_call(
        edge_kernel,
        out_shape=jax.ShapeDtypeStruct((count, width, 128), BF16),
        in_specs=[anywhere(), anywhere()],
        out_specs=vmem(),
        scratch_shapes=[
            pltpu.SMEM((count,), jnp.int32),
            pltpu.VMEM(start_block.shape, F32),
            pltpu.SemaphoreType.DMA((2,)),
        ],
        compiler_params=pltpu.CompilerParams(vmem_limit_bytes=2 * MIB),
        name="edges",
    )(in_hbm(boundary), in_hbm(start_block))


def hold_kernel(w_ref, held_ref, keep_ref, sem):
    copy = pltpu.make_async_copy(w_ref, held_ref, sem)
    copy.start()
    copy.wait()
    ones = jnp.ones((16, w_ref.shape[1]), BF16)
    for i in range(w_ref.shape[0]):
        degree = jnp.dot(ones, held_ref[i], preferred_element_type=F32)
        keep_ref[i] = 1.0 - degree[0:8] * 0.125


def hold_weights(tiles):
    return pl.pallas_call(
        hold_kernel,
        out_shape=(
            jax.ShapeDtypeStruct(tiles.shape, tiles.dtype),
            jax.ShapeDtypeStruct((tiles.shape[0], 8, tiles.shape[2]), F32),
        ),
        in_specs=[anywhere()],
        out_specs=(vmem(), vmem()),
        scratch_shapes=[pltpu.SemaphoreType.DMA],
        compiler_params=pltpu.CompilerParams(vmem_limit_bytes=8 * MIB),
        cost_estimate=pl.CostEstimate(
            flops=0, bytes_accessed=4 * tiles.size, transcendentals=0
        ),
        name="hold_weights",
    )(in_hbm(tiles))


def partners_along(block, axis):
    count = lax.axis_size(axis)

    def pairs(first):
        lows = range(first, count - 1, 2)
        return [(i, i + 1) for i in lows] + [(i + 1, i) for i in lows]

    other = lax.ppermute(block, axis, pairs(1))
    return other, lax.ppermute(block, axis, pairs(0))


def near_kernel(own_ref, mid_ref, pool_ref, sem):
    blocks, listed = own_ref.shape[0], mid_ref.shape[0]
    copies = [
        pltpu.make_async_copy(own_ref, pool_ref.at[pl.ds(0, blocks)], sem.at[0]),
        pltpu.make_async_copy(mid_ref, pool_ref.at[pl.ds(blocks, listed)], sem.at[1]),
    ]
    for copy in copies:
        copy.start()
    for copy in copies:
        copy.wait()


def near_pool(own, mid):
    total = own.shape[0] + 3 * mid.shape[0]
    return pl.pallas_call(
        near_kernel,
        out_shape=jax.ShapeDtypeStruct((total, *own.shape[1:]), own.dtype),
        in_specs=[anywhere(), anywhere()],
        out_specs=vmem(),
        scratch_shapes=[pltpu.SemaphoreType.DMA((2,))],
        compiler_params=pltpu.CompilerParams(vmem_limit_bytes=8 * MIB),
        cost_estimate=pl.CostEstimate(
            flops=0, bytes_accessed=4 * (own.size + mid.size), transcendentals=0
        ),
        name="near_pool",
    )(own, mid)


def halo(own, edge):
    block = edge
    for axis in ("tz", "ty"):
        block = jnp.concatenate([block, *partners_along(block, axis)], axis=0)
    other, partner = partners_along(block, "tx")
    return near_pool(own, block), partner, other


def fill_far(pool_ref, far_refs, sem):
    listed = far_refs[0].shape[0]
    base = pool_ref.shape[0] - 2 * listed
    copies = []
    for j, ref in enumerate(far_refs):
        copies.append(
            pltpu.make_async_copy(ref, pool_ref.at[pl.ds(base + j * listed, listed)], sem.at[j])
        )
        copies[-1].start()
    for copy in copies:
        copy.wait()


def pool_index(codes, blocks, listed):
    place = codes - blocks
    offset = place // listed
    index = jnp.zeros_like(codes)
    for axis, step in (("tx", 9), ("ty", 3), ("tz", 1)):
        way = offset // step % 3
        even = lax.axis_index(axis) % 2 == 0
        last = jnp.where(even, 0, 2) if axis == "tx" else jnp.where(even, 2, 0)
        index = index * 3 + jnp.where(way == 1, 0, jnp.where(way == last, 2, 1))
    return jnp.where(codes < blocks, codes, blocks + index * listed + place % listed)


def gather_sum(table_ref, pool_ref, w_ref, slots, i):
    picked = [pool_ref[table_ref[i * slots + s]] for s in range(slots)]
    return jnp.dot(jnp.concatenate(picked, axis=1), w_ref[i], preferred_element_type=F32)


def first_row(slots, table_ref, x_ref, w_ref, keep_ref, pool_ref, i, lanes):
    out = gather_sum(table_ref, pool_ref, w_ref, slots, i) * 0.125
    keep = keep_ref[i, 0:1]
    mixed = x_ref[:, lanes] * keep + out
    step = (mixed - pool_ref[i].astype(F32) * SHARE).astype(BF16)
    return mixed, mixed * keep + out * SHARE, step


def listed_kernel(
    slots, table_ref, x_ref, w_ref, keep_ref, _, partner_ref, other_ref,
    edge_ref, pool_ref, sem,
):
    fill_far(pool_ref, (partner_ref, other_ref), sem)
    first = w_ref.shape[0] * slots
    for j in range(edge_ref.shape[0]):
        i = table_ref[first + j]
        lanes = pl.ds(pl.multiple_of(i * 128, 128), 128)
        edge_ref[j] = first_row(slots, table_ref, x_ref, w_ref, keep_ref, pool_ref, i, lanes)[2]


def listed_rows(table, count, start_block, weights, keep, far):
    blocks, depth, size = weights.shape
    width = start_block.shape[0]
    return pl.pallas_call(
        functools.partial(listed_kernel, depth // size),
        out_shape=(
            jax.ShapeDtypeStruct((count, width, size), BF16),
            jax.ShapeDtypeStruct(far[0].shape, BF16),
        ),
        in_specs=[smem()] + [vmem()] * 4 + [anywhere()] * 2,
        out_specs=(vmem(),) * 2,
        scratch_shapes=[pltpu.SemaphoreType.DMA((2,))],
        input_output_aliases={4: 1},
        compiler_params=pltpu.CompilerParams(vmem_limit_bytes=16 * MIB),
        name="listed_rows",
    )(table, start_block, weights, keep, *far)


def first_kernel(
    slots, table_ref, x_ref, w_ref, keep_ref, pool_ref, mixed_ref, base_ref, step_ref
):
    for i in range(w_ref.shape[0]):
        lanes = slice(i * 128, (i + 1) * 128)
        mixed_ref[i], base_ref[i], step_ref[i] = first_row(
            slots, table_ref, x_ref, w_ref, keep_ref, pool_ref, i, lanes
        )


def first_step(table, start_block, weights, keep, pool):
    blocks, depth, size = weights.shape
    width = start_block.shape[0]
    shape = (blocks, width, size)
    return pl.pallas_call(
        functools.partial(first_kernel, depth // size),
        out_shape=(
            jax.ShapeDtypeStruct(shape, F32),
            jax.ShapeDtypeStruct(shape, F32),
            jax.ShapeDtypeStruct(shape, BF16),
        ),
        in_specs=[smem()] + [vmem()] * 4,
        out_specs=(vmem(),) * 3,
        compiler_params=pltpu.CompilerParams(vmem_limit_bytes=16 * MIB),
        cost_estimate=pl.CostEstimate(
            flops=2 * width * blocks * depth * size,
            bytes_accessed=2 * weights.size,
            transcendentals=0,
        ),
        name="first_step",
    )(table, start_block, weights, keep, pool)


def gram_kernel(mixed_ref, gram_ref):
    total = None
    for i in range(mixed_ref.shape[0]):
        part = dot_nt(mixed_ref[i], mixed_ref[i])
        total = part if total is None else total + part
    gram_ref[...] = total


def local_gram(mixed):
    blocks, width, _ = mixed.shape
    return pl.pallas_call(
        gram_kernel,
        out_shape=jax.ShapeDtypeStruct((width, width), F32),
        in_specs=[vmem()],
        out_specs=vmem(),
        compiler_params=pltpu.CompilerParams(vmem_limit_bytes=8 * MIB),
        cost_estimate=pl.CostEstimate(
            flops=12 * blocks * 128 * width * width,
            bytes_accessed=4 * blocks * 128 * width,
            transcendentals=0,
        ),
        name="first_gram",
    )(mixed)


def second_kernel(
    slots, table_ref, base_ref, w_ref, gram_ref, _, partner_ref, other_ref,
    out_ref, both_ref, pool_ref, wide, sem,
):
    fill_far(pool_ref, (partner_ref, other_ref), sem)
    for i in range(w_ref.shape[0]):
        mixed = base_ref[i] + gather_sum(table_ref, pool_ref, w_ref, slots, i) * 0.125
        out_ref[i] = mixed
        wide[:, i * 128:(i + 1) * 128] = mixed
    both_ref[...] = jnp.concatenate([gram_ref[...], dot_nt(wide[...], wide[...])], axis=1)


def second_step(table, base, weights, gram, far):
    blocks, width, _ = base.shape
    return pl.pallas_call(
        functools.partial(second_kernel, weights.shape[1] // weights.shape[2]),
        out_shape=(
            jax.ShapeDtypeStruct((blocks, width, 128), F32),
            jax.ShapeDtypeStruct((width, 2 * width), F32),
            jax.ShapeDtypeStruct(far[0].shape, BF16),
        ),
        in_specs=[smem()] + [vmem()] * 4 + [anywhere()] * 2,
        out_specs=(vmem(),) * 3,
        scratch_shapes=[
            pltpu.VMEM((width, blocks * 128), F32),
            pltpu.SemaphoreType.DMA((2,)),
        ],
        input_output_aliases={4: 2},
        compiler_params=pltpu.CompilerParams(vmem_limit_bytes=16 * MIB),
        name="second_step",
    )(table, base, weights, gram, *far)[:2]


def sum_over_devices(values):
    rows, lanes = values.shape
    along, deep, line = (lax.axis_size(axis) for axis in ("tx", "tz", "ty"))
    shape = (rows // along, lanes)
    parts = jnp.broadcast_to(values.reshape(along, 1, *shape), (along, deep, *shape))
    parts = lax.all_to_all(parts.reshape(along * deep, *shape), PLANE, 0, 0)
    mine = jnp.sum(parts, axis=0)
    parts = lax.all_to_all(jnp.broadcast_to(mine[None], (line, *shape)), "ty", 0, 0)
    mine = jnp.sum(parts, axis=0)
    parts = lax.all_to_all(jnp.broadcast_to(mine[None], (along, *shape)), "tx", 0, 0)
    return parts.reshape(rows, lanes)


def finish_kernel(root_scale, gram_ref, mixed_ref, basis_ref, rfactor_ref):
    width, lanes = gram_ref.shape
    tiles = width // PANEL
    lane = lax.broadcasted_iota(jnp.int32, (PANEL, lanes), 1)
    row = lax.broadcasted_iota(jnp.int32, (PANEL, lanes), 0)
    first = lane < width
    own = jnp.where(first, lane, lane - width)
    upper = [gram_ref[t * PANEL:(t + 1) * PANEL, :] for t in range(tiles)]
    inverse = [(own == row + t * PANEL).astype(F32) for t in range(tiles)]
    pivots = []

    def spread_row(tile, r):
        return jnp.broadcast_to(tile[r:r + 1], tile.shape)

    for p in range(tiles):
        columns = []
        for j in range(PANEL):
            lane_of = jnp.where(first, 0, width) + (p * PANEL + j)
            columns.append([
                jnp.take_along_axis(upper[t], lane_of, axis=1, mode="promise_in_bounds")
                if t >= p else None
                for t in range(tiles)
            ])
        corner = [[spread_row(columns[j][p], i) for j in range(i + 1)] for i in range(PANEL)]
        up_rows = [spread_row(upper[p], j) for j in range(PANEL)]
        inv_rows = [spread_row(inverse[p], j) for j in range(PANEL)]
        factor = [[None] * PANEL for _ in range(PANEL)]
        recip = []
        pivot = corner[0][0]
        for j in range(PANEL):
            recip.append(1.0 / corner[j][j])
            pivot = jnp.where(row == j, corner[j][j], pivot)
            for i in range(j + 1, PANEL):
                factor[i][j] = corner[i][j] * recip[j]
            for i in range(j + 1, PANEL):
                for m in range(j + 1, i + 1):
                    corner[i][m] = corner[i][m] - factor[i][j] * corner[m][j]
        pivots.append(pivot)
        for j in range(PANEL):
            for m in range(j + 1, PANEL):
                up_rows[m] = up_rows[m] - factor[m][j] * up_rows[j]
                inv_rows[m] = inv_rows[m] - factor[m][j] * inv_rows[j]
        for t in range(p, tiles):
            left = []
            for j in range(PANEL):
                column = columns[j][t]
                for m in range(j):
                    column = column - left[m] * corner[j][m]
                left.append(column * recip[j])
            if t == p:
                left = [jnp.where(row > j, left[j], 0.0) for j in range(PANEL)]
            for j in range(PANEL):
                upper[t] = upper[t] - left[j] * up_rows[j]
                inverse[t] = inverse[t] - left[j] * inv_rows[j]
    scale = [lax.rsqrt(pivot) for pivot in pivots]
    upper = jnp.concatenate([a * b for a, b in zip(upper, scale)], axis=0)
    inverse = jnp.concatenate([a * b for a, b in zip(inverse, scale)], axis=0)
    rid = lax.broadcasted_iota(jnp.int32, (width, width), 0)
    cid = lax.broadcasted_iota(jnp.int32, (width, width), 1)
    lower_t = jnp.where(cid >= rid, upper[:, width:], 0.0)
    rfactor = dot_nt(lower_t, inverse[:, :width])
    rfactor_ref[...] = jnp.where(cid >= rid, rfactor, 0.0)
    solve = inverse[:, width:] * root_scale
    for i in range(mixed_ref.shape[0]):
        basis_ref[:, i * 128:(i + 1) * 128] = jnp.dot(
            solve, mixed_ref[i], precision=HIGHEST, preferred_element_type=F32
        )


def finish(gram, mixed, root_scale):
    blocks, width, lanes = mixed.shape
    return pl.pallas_call(
        functools.partial(finish_kernel, root_scale),
        out_shape=(
            jax.ShapeDtypeStruct((width, blocks * lanes), F32),
            jax.ShapeDtypeStruct((width, width), F32),
        ),
        in_specs=[vmem(), vmem()],
        out_specs=(vmem(), vmem()),
        compiler_params=pltpu.CompilerParams(vmem_limit_bytes=16 * MIB),
        name="finish",
    )(gram, mixed)


def per_device(start_block, weights, neighbours, boundary):
    points = start_block.shape[1]
    blocks, slots, size, _ = weights.shape
    devices = lax.axis_size("tx") * lax.axis_size("ty") * lax.axis_size("tz")
    root_scale = float(points * devices) ** 0.5
    tiles, keep = hold_weights(weights.reshape(blocks, slots * size, size))
    listed = boundary.shape[0]
    index = pool_index(neighbours, blocks, listed)
    table = jnp.concatenate([index.reshape(-1), boundary])
    own = jnp.swapaxes(start_block.reshape(-1, blocks, size), 0, 1).astype(BF16)
    far = halo(own, take_edges(boundary, start_block))
    edge, pool = listed_rows(table, listed, start_block, tiles, keep, far)
    mixed, base, step = first_step(table, start_block, tiles, keep, pool)
    far = halo(step, edge)
    gram = local_gram(mixed)
    mixed, both = second_step(table, base, tiles, gram, far)
    return finish(sum_over_devices(both), mixed, root_scale)


def solution(mesh):
    placed = (
        P(None, ("tx", "ty", "tz")),
        P(("tx", "ty", "tz"), None, None, None),
        P(("tx", "ty", "tz"), None),
        P(("tx", "ty", "tz")),
    )
    return jax.shard_map(
        per_device,
        mesh=mesh,
        in_specs=placed,
        out_specs=(P(None, ("tx", "ty", "tz")), P()),
        check_vma=False,
    )
```

```python
import functools

import jax
import jax.numpy as jnp
from jax import lax
from jax.experimental import pallas as pl
from jax.experimental.pallas import tpu as pltpu
from jax.sharding import PartitionSpec as P

F32 = jnp.float32
BF16 = jnp.bfloat16
HIGHEST = lax.Precision.HIGHEST
PLANE = ("tx", "tz")
MIB = 1 << 20
PANEL = 8
SHARE = 0.875
FIRST_ORDER = ("tx", "ty")
SECOND_ORDER = ("tx",)


def vmem():
    return pl.BlockSpec(memory_space=pltpu.VMEM)


def smem():
    return pl.BlockSpec(memory_space=pltpu.SMEM)


def anywhere():
    return pl.BlockSpec(memory_space=pl.ANY)


def in_hbm(array):
    return pltpu.with_memory_space_constraint(array, pltpu.HBM)


def dot_nt(a, b):
    return lax.dot_general(
        a, b, (((1,), (1,)), ((), ())), precision=HIGHEST, preferred_element_type=F32
    )


def edge_kernel(list_ref, x_ref, edge_ref, bnd_ref, held, sem):
    copies = [
        pltpu.make_async_copy(list_ref, bnd_ref, sem.at[0]),
        pltpu.make_async_copy(x_ref, held, sem.at[1]),
    ]
    for copy in copies:
        copy.start()
    for copy in copies:
        copy.wait()
    for j in range(edge_ref.shape[0]):
        start = pl.multiple_of(bnd_ref[j] * 128, 128)
        edge_ref[j] = held[:, pl.ds(start, 128)].astype(BF16)


def take_edges(boundary, start_block):
    count = boundary.shape[0]
    width = start_block.shape[0]
    return pl.pallas_call(
        edge_kernel,
        out_shape=jax.ShapeDtypeStruct((count, width, 128), BF16),
        in_specs=[anywhere(), anywhere()],
        out_specs=vmem(),
        scratch_shapes=[
            pltpu.SMEM((count,), jnp.int32),
            pltpu.VMEM(start_block.shape, F32),
            pltpu.SemaphoreType.DMA((2,)),
        ],
        compiler_params=pltpu.CompilerParams(vmem_limit_bytes=2 * MIB),
        name="edges",
    )(in_hbm(boundary), in_hbm(start_block))


def hold_kernel(w_ref, held_ref, keep_ref, sem):
    copy = pltpu.make_async_copy(w_ref, held_ref, sem)
    copy.start()
    copy.wait()
    ones = jnp.ones((16, w_ref.shape[1]), BF16)
    for i in range(w_ref.shape[0]):
        degree = jnp.dot(ones, held_ref[i], preferred_element_type=F32)
        keep_ref[i] = 1.0 - degree[0:8] * 0.125


def hold_weights(tiles):
    return pl.pallas_call(
        hold_kernel,
        out_shape=(
            jax.ShapeDtypeStruct(tiles.shape, tiles.dtype),
            jax.ShapeDtypeStruct((tiles.shape[0], 8, tiles.shape[2]), F32),
        ),
        in_specs=[anywhere()],
        out_specs=(vmem(), vmem()),
        scratch_shapes=[pltpu.SemaphoreType.DMA],
        compiler_params=pltpu.CompilerParams(vmem_limit_bytes=8 * MIB),
        cost_estimate=pl.CostEstimate(
            flops=0, bytes_accessed=4 * tiles.size, transcendentals=0
        ),
        name="hold_weights",
    )(in_hbm(tiles))


def partners_along(block, axis):
    count = lax.axis_size(axis)

    def pairs(first):
        lows = range(first, count - 1, 2)
        return [(i, i + 1) for i in lows] + [(i + 1, i) for i in lows]

    other = lax.ppermute(block, axis, pairs(1))
    return other, lax.ppermute(block, axis, pairs(0))


def near_kernel(own_ref, mid_ref, pool_ref, sem):
    blocks, listed = own_ref.shape[0], mid_ref.shape[0]
    copies = [
        pltpu.make_async_copy(own_ref, pool_ref.at[pl.ds(0, blocks)], sem.at[0]),
        pltpu.make_async_copy(mid_ref, pool_ref.at[pl.ds(blocks, listed)], sem.at[1]),
    ]
    for copy in copies:
        copy.start()
    for copy in copies:
        copy.wait()


def near_pool(own, mid):
    total = own.shape[0] + 3 * mid.shape[0]
    return pl.pallas_call(
        near_kernel,
        out_shape=jax.ShapeDtypeStruct((total, *own.shape[1:]), own.dtype),
        in_specs=[anywhere(), anywhere()],
        out_specs=vmem(),
        scratch_shapes=[pltpu.SemaphoreType.DMA((2,))],
        compiler_params=pltpu.CompilerParams(vmem_limit_bytes=8 * MIB),
        cost_estimate=pl.CostEstimate(
            flops=0, bytes_accessed=4 * (own.size + mid.size), transcendentals=0
        ),
        name="near_pool",
    )(own, mid)


def halo(own, edge, partner_first):
    block = edge
    for axis in ("tz", "ty"):
        other, partner = partners_along(block, axis)
        sides = (partner, other) if axis in partner_first else (other, partner)
        block = jnp.concatenate([block, *sides], axis=0)
    other, partner = partners_along(block, "tx")
    return near_pool(own, block), partner, other


def fill_far(pool_ref, far_refs, table_ref, table, sem):
    listed = far_refs[0].shape[0]
    base = pool_ref.shape[0] - 2 * listed
    copies = [pltpu.make_async_copy(table_ref, table, sem.at[2])]
    copies[0].start()
    for j, ref in enumerate(far_refs):
        copies.append(
            pltpu.make_async_copy(ref, pool_ref.at[pl.ds(base + j * listed, listed)], sem.at[j])
        )
        copies[-1].start()
    for copy in copies:
        copy.wait()


def pool_index(codes, blocks, listed, partner_first):
    place = codes - blocks
    offset = place // listed
    index = jnp.zeros_like(codes)
    for axis, step in (("tx", 9), ("ty", 3), ("tz", 1)):
        way = offset // step % 3
        even = lax.axis_index(axis) % 2 == 0
        last = jnp.where(even, 0, 2) if axis in partner_first else jnp.where(even, 2, 0)
        index = index * 3 + jnp.where(way == 1, 0, jnp.where(way == last, 2, 1))
    return jnp.where(codes < blocks, codes, blocks + index * listed + place % listed)


def gather_sum(table_ref, pool_ref, w_ref, slots, i):
    picked = [pool_ref[table_ref[i * slots + s]] for s in range(slots)]
    return jnp.dot(jnp.concatenate(picked, axis=1), w_ref[i], preferred_element_type=F32)


def first_row(slots, table_ref, x_ref, w_ref, keep_ref, pool_ref, i, lanes):
    out = gather_sum(table_ref, pool_ref, w_ref, slots, i) * 0.125
    keep = keep_ref[i, 0:1]
    mixed = x_ref[:, lanes] * keep + out
    step = (mixed - pool_ref[i].astype(F32) * SHARE).astype(BF16)
    return mixed, mixed * keep + out * SHARE, step


def listed_kernel(
    slots, table_ref, x_ref, w_ref, keep_ref, _, partner_ref, other_ref,
    edge_ref, pool_ref, table, sem,
):
    fill_far(pool_ref, (partner_ref, other_ref), table_ref, table, sem)
    first = w_ref.shape[0] * slots
    for j in range(edge_ref.shape[0]):
        i = table[first + j]
        lanes = pl.ds(pl.multiple_of(i * 128, 128), 128)
        edge_ref[j] = first_row(slots, table, x_ref, w_ref, keep_ref, pool_ref, i, lanes)[2]


def listed_rows(table, count, start_block, weights, keep, far):
    blocks, depth, size = weights.shape
    width = start_block.shape[0]
    return pl.pallas_call(
        functools.partial(listed_kernel, depth // size),
        out_shape=(
            jax.ShapeDtypeStruct((count, width, size), BF16),
            jax.ShapeDtypeStruct(far[0].shape, BF16),
        ),
        in_specs=[anywhere()] + [vmem()] * 4 + [anywhere()] * 2,
        out_specs=(vmem(),) * 2,
        scratch_shapes=[
            pltpu.SMEM(table.shape, jnp.int32),
            pltpu.SemaphoreType.DMA((3,)),
        ],
        input_output_aliases={4: 1},
        compiler_params=pltpu.CompilerParams(vmem_limit_bytes=16 * MIB),
        name="listed_rows",
    )(table, start_block, weights, keep, *far)


def first_kernel(
    slots, table_ref, x_ref, w_ref, keep_ref, pool_ref, mixed_ref, base_ref, step_ref
):
    for i in range(w_ref.shape[0]):
        lanes = slice(i * 128, (i + 1) * 128)
        mixed_ref[i], base_ref[i], step_ref[i] = first_row(
            slots, table_ref, x_ref, w_ref, keep_ref, pool_ref, i, lanes
        )


def first_step(table, start_block, weights, keep, pool):
    blocks, depth, size = weights.shape
    width = start_block.shape[0]
    shape = (blocks, width, size)
    return pl.pallas_call(
        functools.partial(first_kernel, depth // size),
        out_shape=(
            jax.ShapeDtypeStruct(shape, F32),
            jax.ShapeDtypeStruct(shape, F32),
            jax.ShapeDtypeStruct(shape, BF16),
        ),
        in_specs=[smem()] + [vmem()] * 4,
        out_specs=(vmem(),) * 3,
        compiler_params=pltpu.CompilerParams(vmem_limit_bytes=16 * MIB),
        cost_estimate=pl.CostEstimate(
            flops=2 * width * blocks * depth * size,
            bytes_accessed=2 * weights.size,
            transcendentals=0,
        ),
        name="first_step",
    )(table, start_block, weights, keep, pool)


def gram_kernel(mixed_ref, gram_ref):
    total = None
    for i in range(mixed_ref.shape[0]):
        part = dot_nt(mixed_ref[i], mixed_ref[i])
        total = part if total is None else total + part
    gram_ref[...] = total


def local_gram(mixed):
    blocks, width, _ = mixed.shape
    return pl.pallas_call(
        gram_kernel,
        out_shape=jax.ShapeDtypeStruct((width, width), F32),
        in_specs=[vmem()],
        out_specs=vmem(),
        compiler_params=pltpu.CompilerParams(vmem_limit_bytes=8 * MIB),
        cost_estimate=pl.CostEstimate(
            flops=12 * blocks * 128 * width * width,
            bytes_accessed=4 * blocks * 128 * width,
            transcendentals=0,
        ),
        name="first_gram",
    )(mixed)


def second_kernel(
    slots, table_ref, base_ref, w_ref, gram_ref, _, partner_ref, other_ref,
    out_ref, both_ref, pool_ref, table, wide, sem,
):
    width = base_ref.shape[1]
    fill_far(pool_ref, (partner_ref, other_ref), table_ref, table, sem)
    for i in range(w_ref.shape[0]):
        mixed = base_ref[i] + gather_sum(table, pool_ref, w_ref, slots, i) * 0.125
        out_ref[i] = mixed
        rest = mixed
        for part in range(3):
            piece = rest.astype(BF16)
            rest = rest - piece.astype(F32)
            wide[part * width:(part + 1) * width, i * 128:(i + 1) * 128] = piece
    product = lax.dot_general(
        wide[...], wide[...], (((1,), (1,)), ((), ())), preferred_element_type=F32
    )
    rows = product[:width] + product[width:2 * width] + product[2 * width:]
    total = rows[:, :width] + rows[:, width:2 * width] + rows[:, 2 * width:]
    both_ref[...] = jnp.concatenate([gram_ref[...], total], axis=1)


def second_step(table, base, weights, gram, far):
    blocks, width, _ = base.shape
    return pl.pallas_call(
        functools.partial(second_kernel, weights.shape[1] // weights.shape[2]),
        out_shape=(
            jax.ShapeDtypeStruct((blocks, width, 128), F32),
            jax.ShapeDtypeStruct((width, 2 * width), F32),
            jax.ShapeDtypeStruct(far[0].shape, BF16),
        ),
        in_specs=[anywhere()] + [vmem()] * 4 + [anywhere()] * 2,
        out_specs=(vmem(),) * 3,
        scratch_shapes=[
            pltpu.SMEM(table.shape, jnp.int32),
            pltpu.VMEM((3 * width, blocks * 128), BF16),
            pltpu.SemaphoreType.DMA((3,)),
        ],
        input_output_aliases={4: 2},
        compiler_params=pltpu.CompilerParams(vmem_limit_bytes=16 * MIB),
        name="second_step",
    )(table, base, weights, gram, *far)[:2]


def sum_over_devices(values):
    rows, lanes = values.shape
    along, deep, line = (lax.axis_size(axis) for axis in ("tx", "tz", "ty"))
    shape = (rows // along, lanes)
    parts = jnp.broadcast_to(values.reshape(along, 1, *shape), (along, deep, *shape))
    parts = lax.all_to_all(parts.reshape(along * deep, *shape), PLANE, 0, 0)
    mine = jnp.sum(parts, axis=0)
    parts = lax.all_to_all(jnp.broadcast_to(mine[None], (line, *shape)), "ty", 0, 0)
    mine = jnp.sum(parts, axis=0)
    parts = lax.all_to_all(jnp.broadcast_to(mine[None], (along, *shape)), "tx", 0, 0)
    return parts.reshape(rows, lanes)


def finish_kernel(root_scale, gram_ref, mixed_ref, basis_ref, rfactor_ref):
    width, lanes = gram_ref.shape
    tiles = width // PANEL
    lane = lax.broadcasted_iota(jnp.int32, (PANEL, lanes), 1)
    row = lax.broadcasted_iota(jnp.int32, (PANEL, lanes), 0)
    first = lane < width
    own = jnp.where(first, lane, lane - width)
    upper = [gram_ref[t * PANEL:(t + 1) * PANEL, :] for t in range(tiles)]
    inverse = [(own == row + t * PANEL).astype(F32) for t in range(tiles)]
    pivots = []

    def spread_row(tile, r):
        return jnp.broadcast_to(tile[r:r + 1], tile.shape)

    for p in range(tiles):
        columns = []
        for j in range(PANEL):
            lane_of = jnp.where(first, 0, width) + (p * PANEL + j)
            columns.append([
                jnp.take_along_axis(upper[t], lane_of, axis=1, mode="promise_in_bounds")
                if t >= p else None
                for t in range(tiles)
            ])
        corner = [[spread_row(columns[j][p], i) for j in range(i + 1)] for i in range(PANEL)]
        up_rows = [spread_row(upper[p], j) for j in range(PANEL)]
        inv_rows = [spread_row(inverse[p], j) for j in range(PANEL)]
        factor = [[None] * PANEL for _ in range(PANEL)]
        recip = []
        pivot = corner[0][0]
        for j in range(PANEL):
            recip.append(1.0 / corner[j][j])
            pivot = jnp.where(row == j, corner[j][j], pivot)
            for i in range(j + 1, PANEL):
                factor[i][j] = corner[i][j] * recip[j]
            for i in range(j + 1, PANEL):
                for m in range(j + 1, i + 1):
                    corner[i][m] = corner[i][m] - factor[i][j] * corner[m][j]
        pivots.append(pivot)
        for j in range(PANEL):
            for m in range(j + 1, PANEL):
                up_rows[m] = up_rows[m] - factor[m][j] * up_rows[j]
                inv_rows[m] = inv_rows[m] - factor[m][j] * inv_rows[j]
        for t in range(p, tiles):
            left = []
            for j in range(PANEL):
                column = columns[j][t]
                for m in range(j):
                    column = column - left[m] * corner[j][m]
                left.append(column * recip[j])
            if t == p:
                left = [jnp.where(row > j, left[j], 0.0) for j in range(PANEL)]
            for j in range(PANEL):
                upper[t] = upper[t] - left[j] * up_rows[j]
                inverse[t] = inverse[t] - left[j] * inv_rows[j]
    scale = [lax.rsqrt(pivot) for pivot in pivots]
    upper = jnp.concatenate([a * b for a, b in zip(upper, scale)], axis=0)
    inverse = jnp.concatenate([a * b for a, b in zip(inverse, scale)], axis=0)
    rid = lax.broadcasted_iota(jnp.int32, (width, width), 0)
    cid = lax.broadcasted_iota(jnp.int32, (width, width), 1)
    lower_t = jnp.where(cid >= rid, upper[:, width:], 0.0)
    rfactor = dot_nt(lower_t, inverse[:, :width])
    rfactor_ref[...] = jnp.where(cid >= rid, rfactor, 0.0)
    solve = inverse[:, width:] * root_scale
    for i in range(mixed_ref.shape[0]):
        basis_ref[:, i * 128:(i + 1) * 128] = jnp.dot(
            solve, mixed_ref[i], precision=HIGHEST, preferred_element_type=F32
        )


def finish(gram, mixed, root_scale):
    blocks, width, lanes = mixed.shape
    return pl.pallas_call(
        functools.partial(finish_kernel, root_scale),
        out_shape=(
            jax.ShapeDtypeStruct((width, blocks * lanes), F32),
            jax.ShapeDtypeStruct((width, width), F32),
        ),
        in_specs=[vmem(), vmem()],
        out_specs=(vmem(), vmem()),
        compiler_params=pltpu.CompilerParams(vmem_limit_bytes=16 * MIB),
        name="finish",
    )(gram, mixed)


def per_device(start_block, weights, neighbours, boundary):
    points = start_block.shape[1]
    blocks, slots, size, _ = weights.shape
    devices = lax.axis_size("tx") * lax.axis_size("ty") * lax.axis_size("tz")
    root_scale = float(points * devices) ** 0.5
    tiles, keep = hold_weights(weights.reshape(blocks, slots * size, size))
    listed = boundary.shape[0]
    tables = []
    for partner_first in (FIRST_ORDER, SECOND_ORDER):
        index = pool_index(neighbours, blocks, listed, partner_first)
        tables.append(jnp.concatenate([index.reshape(-1), boundary]))
    own = jnp.swapaxes(start_block.reshape(-1, blocks, size), 0, 1).astype(BF16)
    far = halo(own, take_edges(boundary, start_block), FIRST_ORDER)
    edge, pool = listed_rows(tables[0], listed, start_block, tiles, keep, far)
    mixed, base, step = first_step(tables[0], start_block, tiles, keep, pool)
    far = halo(step, edge, SECOND_ORDER)
    gram = local_gram(mixed)
    mixed, both = second_step(tables[1], base, tiles, gram, far)
    return finish(sum_over_devices(both), mixed, root_scale)


def solution(mesh):
    placed = (
        P(None, ("tx", "ty", "tz")),
        P(("tx", "ty", "tz"), None, None, None),
        P(("tx", "ty", "tz"), None),
        P(("tx", "ty", "tz")),
    )
    return jax.shard_map(
        per_device,
        mesh=mesh,
        in_specs=placed,
        out_specs=(P(None, ("tx", "ty", "tz")), P()),
        check_vma=False,
    )
```

```python
import functools

import jax
import jax.numpy as jnp
from jax import lax
from jax.experimental import pallas as pl
from jax.experimental.pallas import tpu as pltpu
from jax.sharding import PartitionSpec as P

F32 = jnp.float32
BF16 = jnp.bfloat16
HIGHEST = lax.Precision.HIGHEST
PLANE = ("tx", "tz")
MIB = 1 << 20
PANEL = 8
SHARE = 0.875


def vmem():
    return pl.BlockSpec(memory_space=pltpu.VMEM)


def smem():
    return pl.BlockSpec(memory_space=pltpu.SMEM)


def anywhere():
    return pl.BlockSpec(memory_space=pl.ANY)


def in_hbm(array):
    return pltpu.with_memory_space_constraint(array, pltpu.HBM)


def dot_nt(a, b):
    return lax.dot_general(
        a, b, (((1,), (1,)), ((), ())), precision=HIGHEST, preferred_element_type=F32
    )


def edge_kernel(list_ref, x_ref, edge_ref, bnd_ref, held, sem):
    copies = [
        pltpu.make_async_copy(list_ref, bnd_ref, sem.at[0]),
        pltpu.make_async_copy(x_ref, held, sem.at[1]),
    ]
    for copy in copies:
        copy.start()
    for copy in copies:
        copy.wait()
    for j in range(edge_ref.shape[0]):
        start = pl.multiple_of(bnd_ref[j] * 128, 128)
        edge_ref[j] = held[:, pl.ds(start, 128)].astype(BF16)


def take_edges(boundary, start_block):
    count = boundary.shape[0]
    width = start_block.shape[0]
    return pl.pallas_call(
        edge_kernel,
        out_shape=jax.ShapeDtypeStruct((count, width, 128), BF16),
        in_specs=[anywhere(), anywhere()],
        out_specs=vmem(),
        scratch_shapes=[
            pltpu.SMEM((count,), jnp.int32),
            pltpu.VMEM(start_block.shape, F32),
            pltpu.SemaphoreType.DMA((2,)),
        ],
        compiler_params=pltpu.CompilerParams(vmem_limit_bytes=2 * MIB),
        name="edges",
    )(in_hbm(boundary), in_hbm(start_block))


def hold_kernel(w_ref, held_ref, keep_ref, sem):
    copy = pltpu.make_async_copy(w_ref, held_ref, sem)
    copy.start()
    copy.wait()
    ones = jnp.ones((16, w_ref.shape[1]), BF16)
    for i in range(w_ref.shape[0]):
        degree = jnp.dot(ones, held_ref[i], preferred_element_type=F32)
        keep_ref[i] = 1.0 - degree[0:8] * 0.125


def hold_weights(tiles):
    return pl.pallas_call(
        hold_kernel,
        out_shape=(
            jax.ShapeDtypeStruct(tiles.shape, tiles.dtype),
            jax.ShapeDtypeStruct((tiles.shape[0], 8, tiles.shape[2]), F32),
        ),
        in_specs=[anywhere()],
        out_specs=(vmem(), vmem()),
        scratch_shapes=[pltpu.SemaphoreType.DMA],
        compiler_params=pltpu.CompilerParams(vmem_limit_bytes=8 * MIB),
        cost_estimate=pl.CostEstimate(
            flops=0, bytes_accessed=4 * tiles.size, transcendentals=0
        ),
        name="hold_weights",
    )(in_hbm(tiles))


def partners_along(block, axis):
    count = lax.axis_size(axis)

    def pairs(first):
        lows = range(first, count - 1, 2)
        return [(i, i + 1) for i in lows] + [(i + 1, i) for i in lows]

    other = lax.ppermute(block, axis, pairs(1))
    return other, lax.ppermute(block, axis, pairs(0))


def near_kernel(own_ref, mid_ref, pool_ref, sem):
    blocks, listed = own_ref.shape[0], mid_ref.shape[0]
    copies = [
        pltpu.make_async_copy(own_ref, pool_ref.at[pl.ds(0, blocks)], sem.at[0]),
        pltpu.make_async_copy(mid_ref, pool_ref.at[pl.ds(blocks, listed)], sem.at[1]),
    ]
    for copy in copies:
        copy.start()
    for copy in copies:
        copy.wait()


def near_pool(own, mid):
    total = own.shape[0] + 3 * mid.shape[0]
    return pl.pallas_call(
        near_kernel,
        out_shape=jax.ShapeDtypeStruct((total, *own.shape[1:]), own.dtype),
        in_specs=[anywhere(), anywhere()],
        out_specs=vmem(),
        scratch_shapes=[pltpu.SemaphoreType.DMA((2,))],
        compiler_params=pltpu.CompilerParams(vmem_limit_bytes=8 * MIB),
        cost_estimate=pl.CostEstimate(
            flops=0, bytes_accessed=4 * (own.size + mid.size), transcendentals=0
        ),
        name="near_pool",
    )(own, mid)


def halo(own, edge):
    block = edge
    for axis in ("tz", "ty"):
        block = jnp.concatenate([block, *partners_along(block, axis)], axis=0)
    other, partner = partners_along(block, "tx")
    return near_pool(own, block), partner, other


def fill_far(pool_ref, far_refs, table_ref, table, sem):
    listed = far_refs[0].shape[0]
    base = pool_ref.shape[0] - 2 * listed
    copies = [pltpu.make_async_copy(table_ref, table, sem.at[2])]
    copies[0].start()
    for j, ref in enumerate(far_refs):
        copies.append(
            pltpu.make_async_copy(ref, pool_ref.at[pl.ds(base + j * listed, listed)], sem.at[j])
        )
        copies[-1].start()
    for copy in copies:
        copy.wait()


def pool_index(codes, blocks, listed):
    place = codes - blocks
    offset = place // listed
    index = jnp.zeros_like(codes)
    for axis, step in (("tx", 9), ("ty", 3), ("tz", 1)):
        way = offset // step % 3
        even = lax.axis_index(axis) % 2 == 0
        last = jnp.where(even, 0, 2) if axis == "tx" else jnp.where(even, 2, 0)
        index = index * 3 + jnp.where(way == 1, 0, jnp.where(way == last, 2, 1))
    return jnp.where(codes < blocks, codes, blocks + index * listed + place % listed)


def gather_sum(table_ref, pool_ref, w_ref, slots, i):
    picked = [pool_ref[table_ref[i * slots + s]] for s in range(slots)]
    return jnp.dot(jnp.concatenate(picked, axis=1), w_ref[i], preferred_element_type=F32)


def first_row(slots, table_ref, x_ref, w_ref, keep_ref, pool_ref, i, lanes):
    out = gather_sum(table_ref, pool_ref, w_ref, slots, i) * 0.125
    keep = keep_ref[i, 0:1]
    mixed = x_ref[:, lanes] * keep + out
    step = (mixed - pool_ref[i].astype(F32) * SHARE).astype(BF16)
    return mixed, mixed * keep + out * SHARE, step


def listed_kernel(
    slots, table_ref, x_ref, w_ref, keep_ref, _, partner_ref, other_ref,
    edge_ref, pool_ref, table, sem,
):
    fill_far(pool_ref, (partner_ref, other_ref), table_ref, table, sem)
    first = w_ref.shape[0] * slots
    for j in range(edge_ref.shape[0]):
        i = table[first + j]
        lanes = pl.ds(pl.multiple_of(i * 128, 128), 128)
        edge_ref[j] = first_row(slots, table, x_ref, w_ref, keep_ref, pool_ref, i, lanes)[2]


def listed_rows(table, count, start_block, weights, keep, far):
    blocks, depth, size = weights.shape
    width = start_block.shape[0]
    return pl.pallas_call(
        functools.partial(listed_kernel, depth // size),
        out_shape=(
            jax.ShapeDtypeStruct((count, width, size), BF16),
            jax.ShapeDtypeStruct(far[0].shape, BF16),
        ),
        in_specs=[anywhere()] + [vmem()] * 4 + [anywhere()] * 2,
        out_specs=(vmem(),) * 2,
        scratch_shapes=[
            pltpu.SMEM(table.shape, jnp.int32),
            pltpu.SemaphoreType.DMA((3,)),
        ],
        input_output_aliases={4: 1},
        compiler_params=pltpu.CompilerParams(vmem_limit_bytes=16 * MIB),
        name="listed_rows",
    )(table, start_block, weights, keep, *far)


def first_kernel(
    slots, table_ref, x_ref, w_ref, keep_ref, pool_ref, mixed_ref, base_ref, step_ref
):
    for i in range(w_ref.shape[0]):
        lanes = slice(i * 128, (i + 1) * 128)
        mixed_ref[i], base_ref[i], step_ref[i] = first_row(
            slots, table_ref, x_ref, w_ref, keep_ref, pool_ref, i, lanes
        )


def first_step(table, start_block, weights, keep, pool):
    blocks, depth, size = weights.shape
    width = start_block.shape[0]
    shape = (blocks, width, size)
    return pl.pallas_call(
        functools.partial(first_kernel, depth // size),
        out_shape=(
            jax.ShapeDtypeStruct(shape, F32),
            jax.ShapeDtypeStruct(shape, F32),
            jax.ShapeDtypeStruct(shape, BF16),
        ),
        in_specs=[smem()] + [vmem()] * 4,
        out_specs=(vmem(),) * 3,
        compiler_params=pltpu.CompilerParams(vmem_limit_bytes=16 * MIB),
        cost_estimate=pl.CostEstimate(
            flops=2 * width * blocks * depth * size,
            bytes_accessed=2 * weights.size,
            transcendentals=0,
        ),
        name="first_step",
    )(table, start_block, weights, keep, pool)


def gram_kernel(mixed_ref, gram_ref):
    total = None
    for i in range(mixed_ref.shape[0]):
        part = dot_nt(mixed_ref[i], mixed_ref[i])
        total = part if total is None else total + part
    gram_ref[...] = total


def local_gram(mixed):
    blocks, width, _ = mixed.shape
    return pl.pallas_call(
        gram_kernel,
        out_shape=jax.ShapeDtypeStruct((width, width), F32),
        in_specs=[vmem()],
        out_specs=vmem(),
        compiler_params=pltpu.CompilerParams(vmem_limit_bytes=8 * MIB),
        cost_estimate=pl.CostEstimate(
            flops=12 * blocks * 128 * width * width,
            bytes_accessed=4 * blocks * 128 * width,
            transcendentals=0,
        ),
        name="first_gram",
    )(mixed)


def second_kernel(
    slots, table_ref, base_ref, w_ref, gram_ref, _, partner_ref, other_ref,
    out_ref, both_ref, pool_ref, table, wide, sem,
):
    width = base_ref.shape[1]
    fill_far(pool_ref, (partner_ref, other_ref), table_ref, table, sem)
    for i in range(w_ref.shape[0]):
        mixed = base_ref[i] + gather_sum(table, pool_ref, w_ref, slots, i) * 0.125
        out_ref[i] = mixed
        rest = mixed
        for part in range(3):
            piece = rest.astype(BF16)
            rest = rest - piece.astype(F32)
            wide[part * width:(part + 1) * width, i * 128:(i + 1) * 128] = piece
    product = lax.dot_general(
        wide[...], wide[...], (((1,), (1,)), ((), ())), preferred_element_type=F32
    )
    rows = product[:width] + product[width:2 * width] + product[2 * width:]
    total = rows[:, :width] + rows[:, width:2 * width] + rows[:, 2 * width:]
    both_ref[...] = jnp.concatenate([gram_ref[...], total], axis=1)


def second_step(table, base, weights, gram, far):
    blocks, width, _ = base.shape
    return pl.pallas_call(
        functools.partial(second_kernel, weights.shape[1] // weights.shape[2]),
        out_shape=(
            jax.ShapeDtypeStruct((blocks, width, 128), F32),
            jax.ShapeDtypeStruct((width, 2 * width), F32),
            jax.ShapeDtypeStruct(far[0].shape, BF16),
        ),
        in_specs=[anywhere()] + [vmem()] * 4 + [anywhere()] * 2,
        out_specs=(vmem(),) * 3,
        scratch_shapes=[
            pltpu.SMEM(table.shape, jnp.int32),
            pltpu.VMEM((3 * width, blocks * 128), BF16),
            pltpu.SemaphoreType.DMA((3,)),
        ],
        input_output_aliases={4: 2},
        compiler_params=pltpu.CompilerParams(vmem_limit_bytes=16 * MIB),
        name="second_step",
    )(table, base, weights, gram, *far)[:2]


def sum_over_devices(values):
    rows, lanes = values.shape
    along, deep, line = (lax.axis_size(axis) for axis in ("tx", "tz", "ty"))
    shape = (rows // along, lanes)
    parts = jnp.broadcast_to(values.reshape(along, 1, *shape), (along, deep, *shape))
    parts = lax.all_to_all(parts.reshape(along * deep, *shape), PLANE, 0, 0)
    mine = jnp.sum(parts, axis=0)
    parts = lax.all_to_all(jnp.broadcast_to(mine[None], (line, *shape)), "ty", 0, 0)
    mine = jnp.sum(parts, axis=0)
    parts = lax.all_to_all(jnp.broadcast_to(mine[None], (along, *shape)), "tx", 0, 0)
    return parts.reshape(rows, lanes)


def finish_kernel(root_scale, gram_ref, mixed_ref, basis_ref, rfactor_ref):
    width, lanes = gram_ref.shape
    tiles = width // PANEL
    lane = lax.broadcasted_iota(jnp.int32, (PANEL, lanes), 1)
    row = lax.broadcasted_iota(jnp.int32, (PANEL, lanes), 0)
    first = lane < width
    own = jnp.where(first, lane, lane - width)
    upper = [gram_ref[t * PANEL:(t + 1) * PANEL, :] for t in range(tiles)]
    inverse = [(own == row + t * PANEL).astype(F32) for t in range(tiles)]
    pivots = []

    def spread_row(tile, r):
        return jnp.broadcast_to(tile[r:r + 1], tile.shape)

    for p in range(tiles):
        columns = []
        for j in range(PANEL):
            lane_of = jnp.where(first, 0, width) + (p * PANEL + j)
            columns.append([
                jnp.take_along_axis(upper[t], lane_of, axis=1, mode="promise_in_bounds")
                if t >= p else None
                for t in range(tiles)
            ])
        corner = [[spread_row(columns[j][p], i) for j in range(i + 1)] for i in range(PANEL)]
        up_rows = [spread_row(upper[p], j) for j in range(PANEL)]
        inv_rows = [spread_row(inverse[p], j) for j in range(PANEL)]
        factor = [[None] * PANEL for _ in range(PANEL)]
        recip = []
        pivot = corner[0][0]
        for j in range(PANEL):
            recip.append(1.0 / corner[j][j])
            pivot = jnp.where(row == j, corner[j][j], pivot)
            for i in range(j + 1, PANEL):
                factor[i][j] = corner[i][j] * recip[j]
            for i in range(j + 1, PANEL):
                for m in range(j + 1, i + 1):
                    corner[i][m] = corner[i][m] - factor[i][j] * corner[m][j]
        pivots.append(pivot)
        for j in range(PANEL):
            for m in range(j + 1, PANEL):
                up_rows[m] = up_rows[m] - factor[m][j] * up_rows[j]
                inv_rows[m] = inv_rows[m] - factor[m][j] * inv_rows[j]
        for t in range(p, tiles):
            left = []
            for j in range(PANEL):
                column = columns[j][t]
                for m in range(j):
                    column = column - left[m] * corner[j][m]
                left.append(column * recip[j])
            if t == p:
                left = [jnp.where(row > j, left[j], 0.0) for j in range(PANEL)]
            for j in range(PANEL):
                upper[t] = upper[t] - left[j] * up_rows[j]
                inverse[t] = inverse[t] - left[j] * inv_rows[j]
    scale = [lax.rsqrt(pivot) for pivot in pivots]
    upper = jnp.concatenate([a * b for a, b in zip(upper, scale)], axis=0)
    inverse = jnp.concatenate([a * b for a, b in zip(inverse, scale)], axis=0)
    rid = lax.broadcasted_iota(jnp.int32, (width, width), 0)
    cid = lax.broadcasted_iota(jnp.int32, (width, width), 1)
    lower_t = jnp.where(cid >= rid, upper[:, width:], 0.0)
    rfactor = dot_nt(lower_t, inverse[:, :width])
    rfactor_ref[...] = jnp.where(cid >= rid, rfactor, 0.0)
    solve = inverse[:, width:] * root_scale
    for i in range(mixed_ref.shape[0]):
        basis_ref[:, i * 128:(i + 1) * 128] = jnp.dot(
            solve, mixed_ref[i], precision=HIGHEST, preferred_element_type=F32
        )


def finish(gram, mixed, root_scale):
    blocks, width, lanes = mixed.shape
    return pl.pallas_call(
        functools.partial(finish_kernel, root_scale),
        out_shape=(
            jax.ShapeDtypeStruct((width, blocks * lanes), F32),
            jax.ShapeDtypeStruct((width, width), F32),
        ),
        in_specs=[vmem(), vmem()],
        out_specs=(vmem(), vmem()),
        compiler_params=pltpu.CompilerParams(vmem_limit_bytes=16 * MIB),
        name="finish",
    )(gram, mixed)


def per_device(start_block, weights, neighbours, boundary):
    points = start_block.shape[1]
    blocks, slots, size, _ = weights.shape
    devices = lax.axis_size("tx") * lax.axis_size("ty") * lax.axis_size("tz")
    root_scale = float(points * devices) ** 0.5
    tiles, keep = hold_weights(weights.reshape(blocks, slots * size, size))
    listed = boundary.shape[0]
    index = pool_index(neighbours, blocks, listed)
    table = jnp.concatenate([index.reshape(-1), boundary])
    own = jnp.swapaxes(start_block.reshape(-1, blocks, size), 0, 1).astype(BF16)
    far = halo(own, take_edges(boundary, start_block))
    edge, pool = listed_rows(table, listed, start_block, tiles, keep, far)
    mixed, base, step = first_step(table, start_block, tiles, keep, pool)
    far = halo(step, edge)
    gram = local_gram(mixed)
    mixed, both = second_step(table, base, tiles, gram, far)
    return finish(sum_over_devices(both), mixed, root_scale)


def solution(mesh):
    placed = (
        P(None, ("tx", "ty", "tz")),
        P(("tx", "ty", "tz"), None, None, None),
        P(("tx", "ty", "tz"), None),
        P(("tx", "ty", "tz")),
    )
    return jax.shard_map(
        per_device,
        mesh=mesh,
        in_specs=placed,
        out_specs=(P(None, ("tx", "ty", "tz")), P()),
        check_vma=False,
    )
```

```python
import functools

import jax
import jax.numpy as jnp
from jax import lax
from jax.experimental import pallas as pl
from jax.experimental.pallas import tpu as pltpu
from jax.sharding import PartitionSpec as P

F32 = jnp.float32
BF16 = jnp.bfloat16
HIGHEST = lax.Precision.HIGHEST
PLANE = ("tx", "tz")
MIB = 1 << 20
PANEL = 8
SHARE = 0.875


def vmem():
    return pl.BlockSpec(memory_space=pltpu.VMEM)


def smem():
    return pl.BlockSpec(memory_space=pltpu.SMEM)


def anywhere():
    return pl.BlockSpec(memory_space=pl.ANY)


def in_hbm(array):
    return pltpu.with_memory_space_constraint(array, pltpu.HBM)


def dot_nt(a, b):
    return lax.dot_general(
        a, b, (((1,), (1,)), ((), ())), precision=HIGHEST, preferred_element_type=F32
    )


def edge_kernel(list_ref, x_ref, edge_ref, bnd_ref, held, sem):
    copies = [
        pltpu.make_async_copy(list_ref, bnd_ref, sem.at[0]),
        pltpu.make_async_copy(x_ref, held, sem.at[1]),
    ]
    for copy in copies:
        copy.start()
    for copy in copies:
        copy.wait()
    for j in range(edge_ref.shape[0]):
        start = pl.multiple_of(bnd_ref[j] * 128, 128)
        edge_ref[j] = held[:, pl.ds(start, 128)].astype(BF16)


def take_edges(boundary, start_block):
    count = boundary.shape[0]
    width = start_block.shape[0]
    return pl.pallas_call(
        edge_kernel,
        out_shape=jax.ShapeDtypeStruct((count, width, 128), BF16),
        in_specs=[anywhere(), anywhere()],
        out_specs=vmem(),
        scratch_shapes=[
            pltpu.SMEM((count,), jnp.int32),
            pltpu.VMEM(start_block.shape, F32),
            pltpu.SemaphoreType.DMA((2,)),
        ],
        compiler_params=pltpu.CompilerParams(vmem_limit_bytes=2 * MIB),
        name="edges",
    )(in_hbm(boundary), in_hbm(start_block))


def hold_kernel(w_ref, held_ref, keep_ref, sem):
    copy = pltpu.make_async_copy(w_ref, held_ref, sem)
    copy.start()
    copy.wait()
    ones = jnp.ones((16, w_ref.shape[1]), BF16)
    for i in range(w_ref.shape[0]):
        degree = jnp.dot(ones, held_ref[i], preferred_element_type=F32)
        keep_ref[i] = 1.0 - degree[0:8] * 0.125


def hold_weights(tiles):
    return pl.pallas_call(
        hold_kernel,
        out_shape=(
            jax.ShapeDtypeStruct(tiles.shape, tiles.dtype),
            jax.ShapeDtypeStruct((tiles.shape[0], 8, tiles.shape[2]), F32),
        ),
        in_specs=[anywhere()],
        out_specs=(vmem(), vmem()),
        scratch_shapes=[pltpu.SemaphoreType.DMA],
        compiler_params=pltpu.CompilerParams(vmem_limit_bytes=8 * MIB),
        cost_estimate=pl.CostEstimate(
            flops=0, bytes_accessed=4 * tiles.size, transcendentals=0
        ),
        name="hold_weights",
    )(in_hbm(tiles))


def partners_along(block, axis):
    count = lax.axis_size(axis)

    def pairs(first):
        lows = range(first, count - 1, 2)
        return [(i, i + 1) for i in lows] + [(i + 1, i) for i in lows]

    other = lax.ppermute(block, axis, pairs(1))
    return other, lax.ppermute(block, axis, pairs(0))


def near_kernel(own_ref, mid_ref, pool_ref, sem):
    blocks, listed = own_ref.shape[0], mid_ref.shape[0]
    copies = [
        pltpu.make_async_copy(own_ref, pool_ref.at[pl.ds(0, blocks)], sem.at[0]),
        pltpu.make_async_copy(mid_ref, pool_ref.at[pl.ds(blocks, listed)], sem.at[1]),
    ]
    for copy in copies:
        copy.start()
    for copy in copies:
        copy.wait()


def near_pool(own, mid):
    total = own.shape[0] + 3 * mid.shape[0]
    return pl.pallas_call(
        near_kernel,
        out_shape=jax.ShapeDtypeStruct((total, *own.shape[1:]), own.dtype),
        in_specs=[anywhere(), anywhere()],
        out_specs=vmem(),
        scratch_shapes=[pltpu.SemaphoreType.DMA((2,))],
        compiler_params=pltpu.CompilerParams(vmem_limit_bytes=8 * MIB),
        cost_estimate=pl.CostEstimate(
            flops=0, bytes_accessed=4 * (own.size + mid.size), transcendentals=0
        ),
        name="near_pool",
    )(own, mid)


def halo(own, edge):
    block = edge
    for axis in ("ty", "tz"):
        block = jnp.concatenate([block, *partners_along(block, axis)], axis=0)
    other, partner = partners_along(block, "tx")
    return near_pool(own, block), partner, other


def fill_far(pool_ref, far_refs, table_ref, table, sem):
    listed = far_refs[0].shape[0]
    base = pool_ref.shape[0] - 2 * listed
    copies = [pltpu.make_async_copy(table_ref, table, sem.at[2])]
    copies[0].start()
    for j, ref in enumerate(far_refs):
        copies.append(
            pltpu.make_async_copy(ref, pool_ref.at[pl.ds(base + j * listed, listed)], sem.at[j])
        )
        copies[-1].start()
    for copy in copies:
        copy.wait()


def pool_index(codes, blocks, listed):
    place = codes - blocks
    offset = place // listed
    index = jnp.zeros_like(codes)
    for axis, step in (("tx", 9), ("tz", 1), ("ty", 3)):
        way = offset // step % 3
        even = lax.axis_index(axis) % 2 == 0
        last = jnp.where(even, 0, 2) if axis == "tx" else jnp.where(even, 2, 0)
        index = index * 3 + jnp.where(way == 1, 0, jnp.where(way == last, 2, 1))
    return jnp.where(codes < blocks, codes, blocks + index * listed + place % listed)


def gather_sum(table_ref, pool_ref, w_ref, slots, i):
    picked = [pool_ref[table_ref[i * slots + s]] for s in range(slots)]
    return jnp.dot(jnp.concatenate(picked, axis=1), w_ref[i], preferred_element_type=F32)


def first_row(slots, table_ref, x_ref, w_ref, keep_ref, pool_ref, i, lanes):
    out = gather_sum(table_ref, pool_ref, w_ref, slots, i) * 0.125
    keep = keep_ref[i, 0:1]
    mixed = x_ref[:, lanes] * keep + out
    step = (mixed - pool_ref[i].astype(F32) * SHARE).astype(BF16)
    return mixed, mixed * keep + out * SHARE, step


def listed_kernel(
    slots, table_ref, x_ref, w_ref, keep_ref, _, partner_ref, other_ref,
    edge_ref, pool_ref, table, sem,
):
    fill_far(pool_ref, (partner_ref, other_ref), table_ref, table, sem)
    first = w_ref.shape[0] * slots
    for j in range(edge_ref.shape[0]):
        i = table[first + j]
        lanes = pl.ds(pl.multiple_of(i * 128, 128), 128)
        edge_ref[j] = first_row(slots, table, x_ref, w_ref, keep_ref, pool_ref, i, lanes)[2]


def listed_rows(table, count, start_block, weights, keep, far):
    blocks, depth, size = weights.shape
    width = start_block.shape[0]
    return pl.pallas_call(
        functools.partial(listed_kernel, depth // size),
        out_shape=(
            jax.ShapeDtypeStruct((count, width, size), BF16),
            jax.ShapeDtypeStruct(far[0].shape, BF16),
        ),
        in_specs=[anywhere()] + [vmem()] * 4 + [anywhere()] * 2,
        out_specs=(vmem(),) * 2,
        scratch_shapes=[
            pltpu.SMEM(table.shape, jnp.int32),
            pltpu.SemaphoreType.DMA((3,)),
        ],
        input_output_aliases={4: 1},
        compiler_params=pltpu.CompilerParams(vmem_limit_bytes=16 * MIB),
        name="listed_rows",
    )(table, start_block, weights, keep, *far)


def first_kernel(
    slots, table_ref, x_ref, w_ref, keep_ref, pool_ref, mixed_ref, base_ref, step_ref
):
    for i in range(w_ref.shape[0]):
        lanes = slice(i * 128, (i + 1) * 128)
        mixed_ref[i], base_ref[i], step_ref[i] = first_row(
            slots, table_ref, x_ref, w_ref, keep_ref, pool_ref, i, lanes
        )


def first_step(table, start_block, weights, keep, pool):
    blocks, depth, size = weights.shape
    width = start_block.shape[0]
    shape = (blocks, width, size)
    return pl.pallas_call(
        functools.partial(first_kernel, depth // size),
        out_shape=(
            jax.ShapeDtypeStruct(shape, F32),
            jax.ShapeDtypeStruct(shape, F32),
            jax.ShapeDtypeStruct(shape, BF16),
        ),
        in_specs=[smem()] + [vmem()] * 4,
        out_specs=(vmem(),) * 3,
        compiler_params=pltpu.CompilerParams(vmem_limit_bytes=16 * MIB),
        cost_estimate=pl.CostEstimate(
            flops=2 * width * blocks * depth * size,
            bytes_accessed=2 * weights.size,
            transcendentals=0,
        ),
        name="first_step",
    )(table, start_block, weights, keep, pool)


def gram_kernel(mixed_ref, gram_ref):
    total = None
    for i in range(mixed_ref.shape[0]):
        part = dot_nt(mixed_ref[i], mixed_ref[i])
        total = part if total is None else total + part
    gram_ref[...] = total


def local_gram(mixed):
    blocks, width, _ = mixed.shape
    return pl.pallas_call(
        gram_kernel,
        out_shape=jax.ShapeDtypeStruct((width, width), F32),
        in_specs=[vmem()],
        out_specs=vmem(),
        compiler_params=pltpu.CompilerParams(vmem_limit_bytes=8 * MIB),
        cost_estimate=pl.CostEstimate(
            flops=12 * blocks * 128 * width * width,
            bytes_accessed=4 * blocks * 128 * width,
            transcendentals=0,
        ),
        name="first_gram",
    )(mixed)


def second_kernel(
    slots, table_ref, base_ref, w_ref, gram_ref, _, partner_ref, other_ref,
    out_ref, both_ref, pool_ref, table, wide, sem,
):
    width = base_ref.shape[1]
    fill_far(pool_ref, (partner_ref, other_ref), table_ref, table, sem)
    for i in range(w_ref.shape[0]):
        mixed = base_ref[i] + gather_sum(table, pool_ref, w_ref, slots, i) * 0.125
        out_ref[i] = mixed
        rest = mixed
        for part in range(3):
            piece = rest.astype(BF16)
            rest = rest - piece.astype(F32)
            wide[part * width:(part + 1) * width, i * 128:(i + 1) * 128] = piece
    product = lax.dot_general(
        wide[...], wide[...], (((1,), (1,)), ((), ())), preferred_element_type=F32
    )
    rows = product[:width] + product[width:2 * width] + product[2 * width:]
    total = rows[:, :width] + rows[:, width:2 * width] + rows[:, 2 * width:]
    both_ref[...] = jnp.concatenate([gram_ref[...], total], axis=1)


def second_step(table, base, weights, gram, far):
    blocks, width, _ = base.shape
    return pl.pallas_call(
        functools.partial(second_kernel, weights.shape[1] // weights.shape[2]),
        out_shape=(
            jax.ShapeDtypeStruct((blocks, width, 128), F32),
            jax.ShapeDtypeStruct((width, 2 * width), F32),
            jax.ShapeDtypeStruct(far[0].shape, BF16),
        ),
        in_specs=[anywhere()] + [vmem()] * 4 + [anywhere()] * 2,
        out_specs=(vmem(),) * 3,
        scratch_shapes=[
            pltpu.SMEM(table.shape, jnp.int32),
            pltpu.VMEM((3 * width, blocks * 128), BF16),
            pltpu.SemaphoreType.DMA((3,)),
        ],
        input_output_aliases={4: 2},
        compiler_params=pltpu.CompilerParams(vmem_limit_bytes=16 * MIB),
        name="second_step",
    )(table, base, weights, gram, *far)[:2]


def sum_over_devices(values):
    rows, lanes = values.shape
    along, deep, line = (lax.axis_size(axis) for axis in ("tx", "tz", "ty"))
    shape = (rows // along, lanes)
    parts = jnp.broadcast_to(values.reshape(along, 1, *shape), (along, deep, *shape))
    parts = lax.all_to_all(parts.reshape(along * deep, *shape), PLANE, 0, 0)
    mine = jnp.sum(parts, axis=0)
    parts = lax.all_to_all(jnp.broadcast_to(mine[None], (line, *shape)), "ty", 0, 0)
    mine = jnp.sum(parts, axis=0)
    parts = lax.all_to_all(jnp.broadcast_to(mine[None], (along, *shape)), "tx", 0, 0)
    return parts.reshape(rows, lanes)


def finish_kernel(root_scale, gram_ref, mixed_ref, basis_ref, rfactor_ref):
    width, lanes = gram_ref.shape
    tiles = width // PANEL
    lane = lax.broadcasted_iota(jnp.int32, (PANEL, lanes), 1)
    row = lax.broadcasted_iota(jnp.int32, (PANEL, lanes), 0)
    first = lane < width
    own = jnp.where(first, lane, lane - width)
    upper = [gram_ref[t * PANEL:(t + 1) * PANEL, :] for t in range(tiles)]
    inverse = [(own == row + t * PANEL).astype(F32) for t in range(tiles)]
    pivots = []

    def spread_row(tile, r):
        return jnp.broadcast_to(tile[r:r + 1], tile.shape)

    for p in range(tiles):
        columns = []
        for j in range(PANEL):
            lane_of = jnp.where(first, 0, width) + (p * PANEL + j)
            columns.append([
                jnp.take_along_axis(upper[t], lane_of, axis=1, mode="promise_in_bounds")
                if t >= p else None
                for t in range(tiles)
            ])
        corner = [[spread_row(columns[j][p], i) for j in range(i + 1)] for i in range(PANEL)]
        up_rows = [spread_row(upper[p], j) for j in range(PANEL)]
        inv_rows = [spread_row(inverse[p], j) for j in range(PANEL)]
        factor = [[None] * PANEL for _ in range(PANEL)]
        recip = []
        pivot = corner[0][0]
        for j in range(PANEL):
            recip.append(1.0 / corner[j][j])
            pivot = jnp.where(row == j, corner[j][j], pivot)
            for i in range(j + 1, PANEL):
                factor[i][j] = corner[i][j] * recip[j]
            for i in range(j + 1, PANEL):
                for m in range(j + 1, i + 1):
                    corner[i][m] = corner[i][m] - factor[i][j] * corner[m][j]
        pivots.append(pivot)
        for j in range(PANEL):
            for m in range(j + 1, PANEL):
                up_rows[m] = up_rows[m] - factor[m][j] * up_rows[j]
                inv_rows[m] = inv_rows[m] - factor[m][j] * inv_rows[j]
        for t in range(p, tiles):
            left = []
            for j in range(PANEL):
                column = columns[j][t]
                for m in range(j):
                    column = column - left[m] * corner[j][m]
                left.append(column * recip[j])
            if t == p:
                left = [jnp.where(row > j, left[j], 0.0) for j in range(PANEL)]
            for j in range(PANEL):
                upper[t] = upper[t] - left[j] * up_rows[j]
                inverse[t] = inverse[t] - left[j] * inv_rows[j]
    scale = [lax.rsqrt(pivot) for pivot in pivots]
    upper = jnp.concatenate([a * b for a, b in zip(upper, scale)], axis=0)
    inverse = jnp.concatenate([a * b for a, b in zip(inverse, scale)], axis=0)
    rid = lax.broadcasted_iota(jnp.int32, (width, width), 0)
    cid = lax.broadcasted_iota(jnp.int32, (width, width), 1)
    lower_t = jnp.where(cid >= rid, upper[:, width:], 0.0)
    rfactor = dot_nt(lower_t, inverse[:, :width])
    rfactor_ref[...] = jnp.where(cid >= rid, rfactor, 0.0)
    solve = inverse[:, width:] * root_scale
    for i in range(mixed_ref.shape[0]):
        basis_ref[:, i * 128:(i + 1) * 128] = jnp.dot(
            solve, mixed_ref[i], precision=HIGHEST, preferred_element_type=F32
        )


def finish(gram, mixed, root_scale):
    blocks, width, lanes = mixed.shape
    return pl.pallas_call(
        functools.partial(finish_kernel, root_scale),
        out_shape=(
            jax.ShapeDtypeStruct((width, blocks * lanes), F32),
            jax.ShapeDtypeStruct((width, width), F32),
        ),
        in_specs=[vmem(), vmem()],
        out_specs=(vmem(), vmem()),
        compiler_params=pltpu.CompilerParams(vmem_limit_bytes=16 * MIB),
        name="finish",
    )(gram, mixed)


def per_device(start_block, weights, neighbours, boundary):
    points = start_block.shape[1]
    blocks, slots, size, _ = weights.shape
    devices = lax.axis_size("tx") * lax.axis_size("ty") * lax.axis_size("tz")
    root_scale = float(points * devices) ** 0.5
    tiles, keep = hold_weights(weights.reshape(blocks, slots * size, size))
    listed = boundary.shape[0]
    index = pool_index(neighbours, blocks, listed)
    table = jnp.concatenate([index.reshape(-1), boundary])
    own = jnp.swapaxes(start_block.reshape(-1, blocks, size), 0, 1).astype(BF16)
    far = halo(own, take_edges(boundary, start_block))
    edge, pool = listed_rows(table, listed, start_block, tiles, keep, far)
    mixed, base, step = first_step(table, start_block, tiles, keep, pool)
    far = halo(step, edge)
    gram = local_gram(mixed)
    mixed, both = second_step(table, base, tiles, gram, far)
    return finish(sum_over_devices(both), mixed, root_scale)


def solution(mesh):
    placed = (
        P(None, ("tx", "ty", "tz")),
        P(("tx", "ty", "tz"), None, None, None),
        P(("tx", "ty", "tz"), None),
        P(("tx", "ty", "tz")),
    )
    return jax.shard_map(
        per_device,
        mesh=mesh,
        in_specs=placed,
        out_specs=(P(None, ("tx", "ty", "tz")), P()),
        check_vma=False,
    )
```

```python
import functools

import jax
import jax.numpy as jnp
from jax import lax
from jax.experimental import pallas as pl
from jax.experimental.pallas import tpu as pltpu
from jax.sharding import PartitionSpec as P

F32 = jnp.float32
BF16 = jnp.bfloat16
HIGHEST = lax.Precision.HIGHEST
PLANE = ("tx", "tz")
MIB = 1 << 20
PANEL = 8
SHARE = 0.875


def vmem():
    return pl.BlockSpec(memory_space=pltpu.VMEM)


def smem():
    return pl.BlockSpec(memory_space=pltpu.SMEM)


def anywhere():
    return pl.BlockSpec(memory_space=pl.ANY)


def in_hbm(array):
    return pltpu.with_memory_space_constraint(array, pltpu.HBM)


def dot_nt(a, b):
    return lax.dot_general(
        a, b, (((1,), (1,)), ((), ())), precision=HIGHEST, preferred_element_type=F32
    )


def edge_kernel(list_ref, x_ref, edge_ref, bnd_ref, held, sem):
    copies = [
        pltpu.make_async_copy(list_ref, bnd_ref, sem.at[0]),
        pltpu.make_async_copy(x_ref, held, sem.at[1]),
    ]
    for copy in copies:
        copy.start()
    for copy in copies:
        copy.wait()
    for j in range(edge_ref.shape[0]):
        start = pl.multiple_of(bnd_ref[j] * 128, 128)
        edge_ref[j] = held[:, pl.ds(start, 128)].astype(BF16)


def take_edges(boundary, start_block):
    count = boundary.shape[0]
    width = start_block.shape[0]
    return pl.pallas_call(
        edge_kernel,
        out_shape=jax.ShapeDtypeStruct((count, width, 128), BF16),
        in_specs=[anywhere(), anywhere()],
        out_specs=vmem(),
        scratch_shapes=[
            pltpu.SMEM((count,), jnp.int32),
            pltpu.VMEM(start_block.shape, F32),
            pltpu.SemaphoreType.DMA((2,)),
        ],
        compiler_params=pltpu.CompilerParams(vmem_limit_bytes=2 * MIB),
        name="edges",
    )(in_hbm(boundary), in_hbm(start_block))


def hold_kernel(w_ref, held_ref, keep_ref, sem):
    copy = pltpu.make_async_copy(w_ref, held_ref, sem)
    copy.start()
    copy.wait()
    ones = jnp.ones((16, w_ref.shape[1]), BF16)
    for i in range(w_ref.shape[0]):
        degree = jnp.dot(ones, held_ref[i], preferred_element_type=F32)
        keep_ref[i] = 1.0 - degree[0:8] * 0.125


def hold_weights(tiles):
    return pl.pallas_call(
        hold_kernel,
        out_shape=(
            jax.ShapeDtypeStruct(tiles.shape, tiles.dtype),
            jax.ShapeDtypeStruct((tiles.shape[0], 8, tiles.shape[2]), F32),
        ),
        in_specs=[anywhere()],
        out_specs=(vmem(), vmem()),
        scratch_shapes=[pltpu.SemaphoreType.DMA],
        compiler_params=pltpu.CompilerParams(vmem_limit_bytes=8 * MIB),
        cost_estimate=pl.CostEstimate(
            flops=0, bytes_accessed=4 * tiles.size, transcendentals=0
        ),
        name="hold_weights",
    )(in_hbm(tiles))


def partners_along(block, axis):
    count = lax.axis_size(axis)

    def pairs(first):
        lows = range(first, count - 1, 2)
        return [(i, i + 1) for i in lows] + [(i + 1, i) for i in lows]

    other = lax.ppermute(block, axis, pairs(1))
    return other, lax.ppermute(block, axis, pairs(0))


def near_kernel(own_ref, mid_ref, pool_ref, sem):
    blocks, listed = own_ref.shape[0], mid_ref.shape[0]
    copies = [
        pltpu.make_async_copy(own_ref, pool_ref.at[pl.ds(0, blocks)], sem.at[0]),
        pltpu.make_async_copy(mid_ref, pool_ref.at[pl.ds(blocks, listed)], sem.at[1]),
    ]
    for copy in copies:
        copy.start()
    for copy in copies:
        copy.wait()


def near_pool(own, mid):
    total = own.shape[0] + 3 * mid.shape[0]
    return pl.pallas_call(
        near_kernel,
        out_shape=jax.ShapeDtypeStruct((total, *own.shape[1:]), own.dtype),
        in_specs=[anywhere(), anywhere()],
        out_specs=vmem(),
        scratch_shapes=[pltpu.SemaphoreType.DMA((2,))],
        compiler_params=pltpu.CompilerParams(vmem_limit_bytes=8 * MIB),
        cost_estimate=pl.CostEstimate(
            flops=0, bytes_accessed=4 * (own.size + mid.size), transcendentals=0
        ),
        name="near_pool",
    )(own, mid)


def halo(own, edge):
    block = edge
    for axis in ("tz", "ty"):
        other, partner = partners_along(block, axis)
        sides = (other, partner) if axis == "tz" else (partner, other)
        block = jnp.concatenate([block, *sides], axis=0)
    other, partner = partners_along(block, "tx")
    return near_pool(own, block), partner, other


def fill_far(pool_ref, far_refs, table_ref, table, sem):
    listed = far_refs[0].shape[0]
    base = pool_ref.shape[0] - 2 * listed
    copies = [pltpu.make_async_copy(table_ref, table, sem.at[2])]
    copies[0].start()
    for j, ref in enumerate(far_refs):
        copies.append(
            pltpu.make_async_copy(ref, pool_ref.at[pl.ds(base + j * listed, listed)], sem.at[j])
        )
        copies[-1].start()
    for copy in copies:
        copy.wait()


def pool_index(codes, blocks, listed):
    place = codes - blocks
    offset = place // listed
    index = jnp.zeros_like(codes)
    for axis, step in (("tx", 9), ("ty", 3), ("tz", 1)):
        way = offset // step % 3
        even = lax.axis_index(axis) % 2 == 0
        last = jnp.where(even, 0, 2) if axis != "tz" else jnp.where(even, 2, 0)
        index = index * 3 + jnp.where(way == 1, 0, jnp.where(way == last, 2, 1))
    return jnp.where(codes < blocks, codes, blocks + index * listed + place % listed)


def gather_sum(table_ref, pool_ref, w_ref, slots, i):
    picked = [pool_ref[table_ref[i * slots + s]] for s in range(slots)]
    return jnp.dot(jnp.concatenate(picked, axis=1), w_ref[i], preferred_element_type=F32)


def first_row(slots, table_ref, x_ref, w_ref, keep_ref, pool_ref, i, lanes):
    out = gather_sum(table_ref, pool_ref, w_ref, slots, i) * 0.125
    keep = keep_ref[i, 0:1]
    mixed = x_ref[:, lanes] * keep + out
    step = (mixed - pool_ref[i].astype(F32) * SHARE).astype(BF16)
    return mixed, mixed * keep + out * SHARE, step


def listed_kernel(
    slots, table_ref, x_ref, w_ref, keep_ref, _, partner_ref, other_ref,
    edge_ref, pool_ref, table, sem,
):
    fill_far(pool_ref, (partner_ref, other_ref), table_ref, table, sem)
    first = w_ref.shape[0] * slots
    for j in range(edge_ref.shape[0]):
        i = table[first + j]
        lanes = pl.ds(pl.multiple_of(i * 128, 128), 128)
        edge_ref[j] = first_row(slots, table, x_ref, w_ref, keep_ref, pool_ref, i, lanes)[2]


def listed_rows(table, count, start_block, weights, keep, far):
    blocks, depth, size = weights.shape
    width = start_block.shape[0]
    return pl.pallas_call(
        functools.partial(listed_kernel, depth // size),
        out_shape=(
            jax.ShapeDtypeStruct((count, width, size), BF16),
            jax.ShapeDtypeStruct(far[0].shape, BF16),
        ),
        in_specs=[anywhere()] + [vmem()] * 4 + [anywhere()] * 2,
        out_specs=(vmem(),) * 2,
        scratch_shapes=[
            pltpu.SMEM(table.shape, jnp.int32),
            pltpu.SemaphoreType.DMA((3,)),
        ],
        input_output_aliases={4: 1},
        compiler_params=pltpu.CompilerParams(vmem_limit_bytes=16 * MIB),
        name="listed_rows",
    )(table, start_block, weights, keep, *far)


def first_kernel(
    slots, table_ref, x_ref, w_ref, keep_ref, pool_ref, mixed_ref, base_ref, step_ref
):
    for i in range(w_ref.shape[0]):
        lanes = slice(i * 128, (i + 1) * 128)
        mixed_ref[i], base_ref[i], step_ref[i] = first_row(
            slots, table_ref, x_ref, w_ref, keep_ref, pool_ref, i, lanes
        )


def first_step(table, start_block, weights, keep, pool):
    blocks, depth, size = weights.shape
    width = start_block.shape[0]
    shape = (blocks, width, size)
    return pl.pallas_call(
        functools.partial(first_kernel, depth // size),
        out_shape=(
            jax.ShapeDtypeStruct(shape, F32),
            jax.ShapeDtypeStruct(shape, F32),
            jax.ShapeDtypeStruct(shape, BF16),
        ),
        in_specs=[smem()] + [vmem()] * 4,
        out_specs=(vmem(),) * 3,
        compiler_params=pltpu.CompilerParams(vmem_limit_bytes=16 * MIB),
        cost_estimate=pl.CostEstimate(
            flops=2 * width * blocks * depth * size,
            bytes_accessed=2 * weights.size,
            transcendentals=0,
        ),
        name="first_step",
    )(table, start_block, weights, keep, pool)


def gram_kernel(mixed_ref, gram_ref):
    total = None
    for i in range(mixed_ref.shape[0]):
        part = dot_nt(mixed_ref[i], mixed_ref[i])
        total = part if total is None else total + part
    gram_ref[...] = total


def local_gram(mixed):
    blocks, width, _ = mixed.shape
    return pl.pallas_call(
        gram_kernel,
        out_shape=jax.ShapeDtypeStruct((width, width), F32),
        in_specs=[vmem()],
        out_specs=vmem(),
        compiler_params=pltpu.CompilerParams(vmem_limit_bytes=8 * MIB),
        cost_estimate=pl.CostEstimate(
            flops=12 * blocks * 128 * width * width,
            bytes_accessed=4 * blocks * 128 * width,
            transcendentals=0,
        ),
        name="first_gram",
    )(mixed)


def second_kernel(
    slots, table_ref, base_ref, w_ref, gram_ref, _, partner_ref, other_ref,
    out_ref, both_ref, pool_ref, table, wide, sem,
):
    width = base_ref.shape[1]
    fill_far(pool_ref, (partner_ref, other_ref), table_ref, table, sem)
    for i in range(w_ref.shape[0]):
        mixed = base_ref[i] + gather_sum(table, pool_ref, w_ref, slots, i) * 0.125
        out_ref[i] = mixed
        rest = mixed
        for part in range(3):
            piece = rest.astype(BF16)
            rest = rest - piece.astype(F32)
            wide[part * width:(part + 1) * width, i * 128:(i + 1) * 128] = piece
    product = lax.dot_general(
        wide[...], wide[...], (((1,), (1,)), ((), ())), preferred_element_type=F32
    )
    rows = product[:width] + product[width:2 * width] + product[2 * width:]
    total = rows[:, :width] + rows[:, width:2 * width] + rows[:, 2 * width:]
    both_ref[...] = jnp.concatenate([gram_ref[...], total], axis=1)


def second_step(table, base, weights, gram, far):
    blocks, width, _ = base.shape
    return pl.pallas_call(
        functools.partial(second_kernel, weights.shape[1] // weights.shape[2]),
        out_shape=(
            jax.ShapeDtypeStruct((blocks, width, 128), F32),
            jax.ShapeDtypeStruct((width, 2 * width), F32),
            jax.ShapeDtypeStruct(far[0].shape, BF16),
        ),
        in_specs=[anywhere()] + [vmem()] * 4 + [anywhere()] * 2,
        out_specs=(vmem(),) * 3,
        scratch_shapes=[
            pltpu.SMEM(table.shape, jnp.int32),
            pltpu.VMEM((3 * width, blocks * 128), BF16),
            pltpu.SemaphoreType.DMA((3,)),
        ],
        input_output_aliases={4: 2},
        compiler_params=pltpu.CompilerParams(vmem_limit_bytes=16 * MIB),
        name="second_step",
    )(table, base, weights, gram, *far)[:2]


def sum_over_devices(values):
    rows, lanes = values.shape
    along, deep, line = (lax.axis_size(axis) for axis in ("tx", "tz", "ty"))
    shape = (rows // along, lanes)
    parts = jnp.broadcast_to(values.reshape(along, 1, *shape), (along, deep, *shape))
    parts = lax.all_to_all(parts.reshape(along * deep, *shape), PLANE, 0, 0)
    mine = jnp.sum(parts, axis=0)
    parts = lax.all_to_all(jnp.broadcast_to(mine[None], (line, *shape)), "ty", 0, 0)
    mine = jnp.sum(parts, axis=0)
    parts = lax.all_to_all(jnp.broadcast_to(mine[None], (along, *shape)), "tx", 0, 0)
    return parts.reshape(rows, lanes)


def finish_kernel(root_scale, gram_ref, mixed_ref, basis_ref, rfactor_ref):
    width, lanes = gram_ref.shape
    tiles = width // PANEL
    lane = lax.broadcasted_iota(jnp.int32, (PANEL, lanes), 1)
    row = lax.broadcasted_iota(jnp.int32, (PANEL, lanes), 0)
    first = lane < width
    own = jnp.where(first, lane, lane - width)
    upper = [gram_ref[t * PANEL:(t + 1) * PANEL, :] for t in range(tiles)]
    inverse = [(own == row + t * PANEL).astype(F32) for t in range(tiles)]
    pivots = []

    def spread_row(tile, r):
        return jnp.broadcast_to(tile[r:r + 1], tile.shape)

    for p in range(tiles):
        columns = []
        for j in range(PANEL):
            lane_of = jnp.where(first, 0, width) + (p * PANEL + j)
            columns.append([
                jnp.take_along_axis(upper[t], lane_of, axis=1, mode="promise_in_bounds")
                if t >= p else None
                for t in range(tiles)
            ])
        corner = [[spread_row(columns[j][p], i) for j in range(i + 1)] for i in range(PANEL)]
        up_rows = [spread_row(upper[p], j) for j in range(PANEL)]
        inv_rows = [spread_row(inverse[p], j) for j in range(PANEL)]
        factor = [[None] * PANEL for _ in range(PANEL)]
        recip = []
        pivot = corner[0][0]
        for j in range(PANEL):
            recip.append(1.0 / corner[j][j])
            pivot = jnp.where(row == j, corner[j][j], pivot)
            for i in range(j + 1, PANEL):
                factor[i][j] = corner[i][j] * recip[j]
            for i in range(j + 1, PANEL):
                for m in range(j + 1, i + 1):
                    corner[i][m] = corner[i][m] - factor[i][j] * corner[m][j]
        pivots.append(pivot)
        for j in range(PANEL):
            for m in range(j + 1, PANEL):
                up_rows[m] = up_rows[m] - factor[m][j] * up_rows[j]
                inv_rows[m] = inv_rows[m] - factor[m][j] * inv_rows[j]
        for t in range(p, tiles):
            left = []
            for j in range(PANEL):
                column = columns[j][t]
                for m in range(j):
                    column = column - left[m] * corner[j][m]
                left.append(column * recip[j])
            if t == p:
                left = [jnp.where(row > j, left[j], 0.0) for j in range(PANEL)]
            for j in range(PANEL):
                upper[t] = upper[t] - left[j] * up_rows[j]
                inverse[t] = inverse[t] - left[j] * inv_rows[j]
    scale = [lax.rsqrt(pivot) for pivot in pivots]
    upper = jnp.concatenate([a * b for a, b in zip(upper, scale)], axis=0)
    inverse = jnp.concatenate([a * b for a, b in zip(inverse, scale)], axis=0)
    rid = lax.broadcasted_iota(jnp.int32, (width, width), 0)
    cid = lax.broadcasted_iota(jnp.int32, (width, width), 1)
    lower_t = jnp.where(cid >= rid, upper[:, width:], 0.0)
    rfactor = dot_nt(lower_t, inverse[:, :width])
    rfactor_ref[...] = jnp.where(cid >= rid, rfactor, 0.0)
    solve = inverse[:, width:] * root_scale
    for i in range(mixed_ref.shape[0]):
        basis_ref[:, i * 128:(i + 1) * 128] = jnp.dot(
            solve, mixed_ref[i], precision=HIGHEST, preferred_element_type=F32
        )


def finish(gram, mixed, root_scale):
    blocks, width, lanes = mixed.shape
    return pl.pallas_call(
        functools.partial(finish_kernel, root_scale),
        out_shape=(
            jax.ShapeDtypeStruct((width, blocks * lanes), F32),
            jax.ShapeDtypeStruct((width, width), F32),
        ),
        in_specs=[vmem(), vmem()],
        out_specs=(vmem(), vmem()),
        compiler_params=pltpu.CompilerParams(vmem_limit_bytes=16 * MIB),
        name="finish",
    )(gram, mixed)


def per_device(start_block, weights, neighbours, boundary):
    points = start_block.shape[1]
    blocks, slots, size, _ = weights.shape
    devices = lax.axis_size("tx") * lax.axis_size("ty") * lax.axis_size("tz")
    root_scale = float(points * devices) ** 0.5
    tiles, keep = hold_weights(weights.reshape(blocks, slots * size, size))
    listed = boundary.shape[0]
    index = pool_index(neighbours, blocks, listed)
    table = jnp.concatenate([index.reshape(-1), boundary])
    own = jnp.swapaxes(start_block.reshape(-1, blocks, size), 0, 1).astype(BF16)
    far = halo(own, take_edges(boundary, start_block))
    edge, pool = listed_rows(table, listed, start_block, tiles, keep, far)
    mixed, base, step = first_step(table, start_block, tiles, keep, pool)
    far = halo(step, edge)
    gram = local_gram(mixed)
    mixed, both = second_step(table, base, tiles, gram, far)
    return finish(sum_over_devices(both), mixed, root_scale)


def solution(mesh):
    placed = (
        P(None, ("tx", "ty", "tz")),
        P(("tx", "ty", "tz"), None, None, None),
        P(("tx", "ty", "tz"), None),
        P(("tx", "ty", "tz")),
    )
    return jax.shard_map(
        per_device,
        mesh=mesh,
        in_specs=placed,
        out_specs=(P(None, ("tx", "ty", "tz")), P()),
        check_vma=False,
    )
```
